32 devices in a mesh: section: 4 (over y, core), ep: 8 (over z, x).
Axes of the slice: x: 2, y: 2, z: 4, core: 2. Of those that a mesh axis runs over, the one named last changes fastest.
Arguments:
- rows_in: bfloat16 [4, 64, 7168], P(None, 'ep'), may hold values from -6 to 6
- routes: int32 [4, 4, 64, 2], P('section', None, 'ep'), may hold values from 0 to 3, all different within a row; in each aligned block of 8 rows (0 to 7, 8 to 15, ..., all dimensions but the last counted through in order) at most 4 rows name the same one
- hot_blocks: int32 [4], P('section'), may hold values from 0 to 15
- gains: float32 [4, 7168], P('section'), may hold values from 0.1 to 1.9
- router: bfloat16 [4, 7168, 4], P('section'), may hold values from -0.0625 to 0.0625
- w_gate: bfloat16 [4, 7168, 4096], P('section', None, 'ep'), may hold values from -0.0625 to 0.0625
- w_up: bfloat16 [4, 7168, 4096], P('section', None, 'ep'), may hold values from -0.0625 to 0.0625
- w_down: bfloat16 [4, 4096, 7168], P('section', 'ep'), may hold values from -0.1875 to 0.1875
Outputs:
- section_rows: bfloat16 [4, 4, 64, 7168], P('section', None, 'ep')
- relative_load: float32 [4, 8], P('section', 'ep')
The draws below stay inside these ranges and needn't reach their ends.
Inputs may be any that keep to these rules, and one draw needn't show every extreme that they name: `routes`: in every layer and micro-batch the 8 rows of one device name each expert at most 4 times.
All inputs are finite; a program needn't handle non-finite values.
Results may differ from the reference program's by a relative error of at most 0.025.
Values may be sent and summed in bfloat16 or wider, within the bound.
A program may use at most 128 MiB of HBM per device.

```python
import math
import jax
import jax.numpy as jnp
import numpy as np
from jax import lax

D = 7168
FFW = 1024
BLK = 256
TOP = 2
MICRO = 4
TOK_DEV = 8
CAP = 4
EXPERTS = 4
BLOCKS = 16
LAYERS = 4
TOKENS = 64
N_EP = 8


def touch_ends(result, key, least, top_value):
    longest = result.shape.index(max(result.shape))
    spots = []
    for shift in (0, 1):
        where = [jax.random.randint(jax.random.fold_in(key, axis), (), 0, length) for axis, length in enumerate(result.shape)]
        where[longest] = (where[longest] + shift) % result.shape[longest]
        spots.append(tuple(where))
    return result.at[spots[0]].set(least).at[spots[1]].set(top_value)


def level_of(own_key, extent, cuts, smallest, high):
    gain = 1.0
    for position, shards_of in cuts:
        draws = jax.random.uniform(jax.random.fold_in(jax.random.fold_in(own_key, 6), position), (shards_of,), jnp.float32, smallest / len(cuts), high / len(cuts))
        gain = gain * jnp.repeat(jnp.exp(draws), extent[position] // shards_of).reshape((-1,) + (1,) * (len(extent) - 1 - position))
    return gain


def deal_out(stream_key, own, number, rows, amount, top, limit, slope):
    ranking = jax.random.permutation(stream_key, amount)
    heavy_load, common = shares(amount, rows * top, limit, slope, True), shares(amount, rows * top, limit, slope, False)
    places = jnp.arange(amount)

    def named(lengths, turn):
        used = int((lengths > 0).sum())
        fixed = max(1, used // 4)
        moved = fixed + (places - fixed + turn * (used - fixed)) % max(1, amount - fixed)
        return jnp.zeros((amount,), jnp.int32).at[ranking[jnp.where(places < fixed, places, moved)]].set(jnp.asarray(lengths, jnp.int32))

    lengths = jnp.where(number % 4 == 0, named(heavy_load, number // 4), named(common, number - number // 4 - 1))
    mixed = jax.random.permutation(jax.random.fold_in(own, 3), amount)
    donor, sink = mixed[0:amount // 2 * 2:2], mixed[1:amount // 2 * 2:2]
    room = jnp.minimum(lengths[donor] - 1, limit - lengths[sink]) // 2
    room = jnp.where((donor == ranking[0]) | (sink == ranking[0]) | (lengths[sink] == 0), 0, jnp.maximum(room, 0))
    moved = jax.random.randint(jax.random.fold_in(own, 4), (amount // 2,), 0, 1 << 20) % (room + 1)
    lengths = lengths.at[donor].add(-moved).at[sink].add(moved)
    members = jnp.searchsorted(jnp.cumsum(lengths), jnp.arange(rows * top), side="right").astype(jnp.int32)
    table = members.reshape(top, rows).T
    table = table[jax.random.permutation(jax.random.fold_in(own, 1), rows)]
    turn = jax.random.randint(jax.random.fold_in(own, 2), (rows, 1), 0, top)
    return jnp.take_along_axis(table, (jnp.arange(top)[None, :] + turn) % top, axis=1)


def shares(number_of, total, bound, skew, full):
    weights = [(1 << 20) // math.isqrt(grade ** skew) + 1 for grade in range(1, number_of + 1)]
    largest = bound if full else min(bound, max(-(-total // number_of), total * weights[0] // sum(weights)))
    least = 1 if total - largest >= number_of - 1 else 0
    holding, spare = [largest] + [least] * (number_of - 1), total - largest - least * (number_of - 1)
    while spare > 0:
        candidates = [i for i in range(1, number_of) if holding[i] < largest] or [i for i in range(1, number_of) if holding[i] < bound]
        pool, left = sum([weights[i] for i in candidates]), spare
        for i in candidates:
            extra = min(bound - holding[i], max(1, left * weights[i] // pool), spare)
            holding[i] = holding[i] + extra
            spare = spare - extra
    return np.array(holding)


def scatter_about(stream_key, shape, deviation, most, split=(), kind=jnp.bfloat16):
    gain = level_of(stream_key, shape, split, -0.22, 0.18) if split else 1.0
    result = jax.random.normal(stream_key, shape, jnp.float32) * deviation * gain
    return jnp.minimum(jnp.maximum(result, -most), most).astype(kind)


def setup_inputs(seed: int = 0) -> dict:
    key_of = jax.random.split(jax.random.key(seed), 9)
    rows_in = scatter_about(key_of[0], (MICRO, TOKENS, D), 1.0, 6.0, ((1, 8),))
    routes_keys = jax.random.split(jax.random.fold_in(key_of[1], 1), LAYERS * MICRO * TOKENS // TOK_DEV)
    routes_turns = jax.random.permutation(jax.random.fold_in(key_of[1], 3), LAYERS * MICRO * TOKENS // TOK_DEV)
    routes = jax.vmap(lambda own, number: deal_out(jax.random.fold_in(key_of[1], 2), own, number, TOK_DEV, EXPERTS, TOP, CAP, 2))(routes_keys, routes_turns).reshape((LAYERS, MICRO, TOKENS, TOP))
    hot_blocks = touch_ends(jax.random.randint(key_of[2], (LAYERS,), 0, BLOCKS), jax.random.fold_in(key_of[2], 1), 0, BLOCKS - 1).astype(jnp.int32)
    gains = jnp.clip(1.0 + 0.18 * jax.random.normal(key_of[3], (LAYERS, D), jnp.float32), 0.1, 1.9)
    router = scatter_about(key_of[4], (LAYERS, D, EXPERTS), D ** -0.5, 0.0625, ((0, 4),))
    w_gate = scatter_about(key_of[5], (LAYERS, D, EXPERTS * FFW), D ** -0.5, 0.0625, ((0, 4), (2, 8)))
    w_up = scatter_about(key_of[6], (LAYERS, D, EXPERTS * FFW), D ** -0.5, 0.0625, ((0, 4), (2, 8)))
    w_down = scatter_about(key_of[7], (LAYERS, EXPERTS * FFW, D), FFW ** -0.5, 0.1875, ((0, 4), (1, 8)))
    return {"rows_in": rows_in, "routes": routes, "hot_blocks": hot_blocks, "gains": gains, "router": router, "w_gate": w_gate, "w_up": w_up, "w_down": w_down}


def apply_layer(rows, route_ids, hot_index, norm_gain, router_w, gate_w, up_w, down_w, down_float):
    rows_float = rows.astype(jnp.float32)
    mean_square = lax.optimization_barrier(jnp.mean(rows_float * rows_float, axis=-1, keepdims=True))
    normed = (rows_float * lax.rsqrt(mean_square + 1e-06) * norm_gain).astype(jnp.bfloat16)
    scores = jax.nn.sigmoid(jnp.dot(normed, router_w, preferred_element_type=jnp.float32))
    chosen = jnp.take_along_axis(scores, route_ids, axis=1)
    gate_weights = 2.5 * chosen / lax.optimization_barrier(jnp.sum(chosen, axis=1, keepdims=True))
    gate_value = jnp.dot(normed, gate_w, preferred_element_type=jnp.float32)
    up_value = jnp.dot(normed, up_w, preferred_element_type=jnp.float32)
    activation = (jax.nn.silu(gate_value) * up_value).astype(jnp.bfloat16)
    column_block = jnp.arange(EXPERTS * FFW, dtype=jnp.int32) // BLK
    home_act = jnp.where((column_block != hot_index)[None, :], activation, jnp.zeros_like(activation))
    token_count = rows.shape[0]
    home_part = jnp.einsum('tpc,pcd->tpd', home_act.reshape(token_count, N_EP, 2 * BLK).astype(jnp.float32), down_float)
    home_part = lax.optimization_barrier(home_part.astype(jnp.bfloat16)).astype(jnp.float32)
    halves = home_part.reshape(token_count, EXPERTS, 2, D)
    pair_sum = halves[:, :, 0, :] + halves[:, :, 1, :]
    hot_act = lax.dynamic_slice_in_dim(activation, (hot_index * BLK).astype(jnp.int32), BLK, 1)
    hot_down = lax.dynamic_slice_in_dim(down_w, (hot_index * BLK).astype(jnp.int32), BLK, 0)
    hot_part = jnp.dot(hot_act, hot_down, preferred_element_type=jnp.float32)
    hot_part = lax.optimization_barrier(hot_part.astype(jnp.bfloat16)).astype(jnp.float32)
    one_hot = (route_ids[:, :, None] == jnp.arange(EXPERTS, dtype=jnp.int32)[None, None, :]).astype(jnp.float32)
    selected = jnp.einsum('tke,ted->tkd', one_hot, pair_sum, precision=lax.Precision.HIGHEST)
    hot_expert = hot_index // (FFW // BLK)
    is_hot = (route_ids == hot_expert).astype(jnp.float32)[:, :, None]
    routed_sum = lax.optimization_barrier(jnp.sum(gate_weights[:, :, None] * (selected + is_hot * hot_part[:, None, :]), axis=1))
    return (rows_float + routed_sum).astype(jnp.bfloat16)

def layer_load(route_layer, hot_index):
    member = (route_layer[..., None] == jnp.arange(EXPERTS, dtype=jnp.int32)).astype(jnp.int32)
    expert_total = lax.optimization_barrier(jnp.sum(member, axis=(0, 1, 2)))
    device_ids = jnp.arange(N_EP, dtype=jnp.int32)
    home_units = expert_total[device_ids // 2] * (2 - (device_ids == hot_index // 2).astype(jnp.int32))
    hot_expert = hot_index // (FFW // BLK)
    per_token = lax.optimization_barrier(jnp.sum((route_layer == hot_expert).astype(jnp.int32), axis=(0, 2)))
    own_units = lax.optimization_barrier(jnp.sum(per_token.reshape(N_EP, TOK_DEV), axis=1))
    unit_count = (home_units + own_units).astype(jnp.float32)
    return unit_count / float(MICRO * TOK_DEV * TOP * (FFW // BLK))

def reference(rows_in, routes, hot_blocks, gains, router, w_gate, w_up, w_down):
    current = rows_in
    layer_rows = []
    load_rows = []
    for layer_index in range(LAYERS):
        down_float = w_down[layer_index].astype(jnp.float32).reshape(N_EP, 2 * BLK, D)
        hot_index = hot_blocks[layer_index]
        next_list = []
        for micro_index in range(MICRO):
            next_list.append(apply_layer(current[micro_index], routes[layer_index, micro_index], hot_index, gains[layer_index], router[layer_index], w_gate[layer_index], w_up[layer_index], w_down[layer_index], down_float))
        current = jnp.stack(next_list)
        layer_rows.append(current)
        load_rows.append(layer_load(routes[layer_index], hot_index))
    return (jnp.stack(layer_rows), jnp.stack(load_rows))
```

```python
import functools

import jax
import jax.numpy as jnp
from jax import lax
from jax.experimental import pallas as pl
from jax.experimental.pallas import tpu as pltpu
from jax.sharding import PartitionSpec as P

BLOCKS_PER_EXPERT = 4
MESH = pl.DeviceIdType.MESH
F32 = jnp.float32
BF16 = jnp.bfloat16


def flip(index, mask, count):
    result, bit = 0, 1
    while bit < count:
        digit = (index // bit) % 2
        result = result + bit * ((1 - digit) if mask & bit else digit)
        bit *= 2
    return result


def kernel(
    sections, n, experts, top,
    rows_hbm, routes_ref, hot_ref, gains_ref, router_ref, gate_hbm, up_hbm, down_hbm,
    out_ref, load_ref,
    gate_w, up_w, down_w, xin, send, recv, back, ret, nrm, place_w, pack_t, mix, act, counts, counts_in,
    weight_sem, in_sem, next_sem, disp_send, disp_recv, ret_send, ret_recv, count_send, count_recv,
):
    micro, tok, width = xin.shape
    cap = tok // 2
    lanes = n // experts
    half = width // 2
    chunk = 1024 if width % 1024 == 0 else width
    section = lax.axis_index("section")
    me = lax.axis_index("ep")
    own_expert = me // lanes
    last = sections - 1
    peers = [flip(me, mask, n) for mask in range(n - 1, 0, -1)]

    weights = [
        pltpu.make_async_copy(source, target, weight_sem.at[i])
        for i, (source, target) in enumerate(((gate_hbm, gate_w), (up_hbm, up_w), (down_hbm, down_w)))
    ]

    def entry(m):
        return pltpu.make_async_copy(rows_hbm.at[m], xin.at[m], in_sem.at[m])

    @pl.when(section == 0)
    def _():
        for m in range(micro):
            entry(m).start()

    for copy in weights:
        copy.start()

    barrier = pltpu.get_barrier_semaphore()
    for peer in peers:
        pl.semaphore_signal(barrier, inc=1, device_id=(section, peer), device_id_type=MESH)

    @pl.when(section < last)
    def _():
        pl.semaphore_signal(barrier, inc=1, device_id=(section + 1, me), device_id_type=MESH)

    @pl.when(section > 0)
    def _():
        pl.semaphore_signal(barrier, inc=1, device_id=(section - 1, me), device_id_type=MESH)

    def placement(m, spread, rows):
        slot = lax.broadcasted_iota(jnp.int32, (rows, tok), 0)
        expert, rank = slot // (spread * cap), slot % cap
        routed = (routes_ref[m, 0:1, :] == expert) | (routes_ref[m, 1:2, :] == expert)
        earlier = (
            lax.broadcasted_iota(jnp.int32, (tok, tok), 0) < lax.broadcasted_iota(jnp.int32, (tok, tok), 1)
        ).astype(BF16)
        taken = jnp.dot(routed.astype(BF16), earlier, preferred_element_type=F32)
        return jnp.where(routed & (taken == rank.astype(F32)), 1.0, 0.0)

    held = jnp.zeros((1, 128), F32)
    for m in range(micro):
        pack_t[m] = placement(m, 1, experts * cap).astype(BF16)
        place = placement(m, lanes, 128).T
        place_w[m] = place
        held = held + jnp.sum(place, axis=0, keepdims=True)
    counts[...] = jnp.broadcast_to(held, counts.shape)

    neighbours = (section > 0).astype(jnp.int32) + (section < last).astype(jnp.int32)
    pl.semaphore_wait(barrier, n - 1 + neighbours)

    def count_copy(peer, source, order):
        return pltpu.make_async_remote_copy(
            counts, counts_in.at[source], count_send.at[order], count_recv.at[source],
            device_id=(section, peer), device_id_type=MESH,
        )

    def dispatch(m, peer, order, source):
        return pltpu.make_async_remote_copy(
            send.at[m, peer // lanes], recv.at[m, source], disp_send.at[m, order], disp_recv.at[m, source],
            device_id=(section, peer), device_id_type=MESH,
        )

    def give_back(m, part, peer, order, source):
        columns = pl.ds(part * half, half)
        return pltpu.make_async_remote_copy(
            back.at[m, peer, :, columns], ret.at[m, source, :, columns], ret_send.at[m, part, order], ret_recv.at[m, part, source],
            device_id=(section, peer), device_id_type=MESH,
        )

    def onward(m):
        return pltpu.make_async_remote_copy(
            out_ref.at[m], xin.at[m], next_sem.at[m], in_sem.at[m],
            device_id=(section + 1, me), device_id_type=MESH,
        )

    def start_rows(m):
        entry(m).wait()
        x = xin[m].astype(F32)
        scale = lax.rsqrt(jnp.mean(x * x, axis=-1, keepdims=True) + 1e-06)
        selector = pack_t[m]
        for c in range(0, width, chunk):
            normed = (xin[m, :, c:c + chunk].astype(F32) * scale * gains_ref[:, c:c + chunk]).astype(BF16)
            nrm[m, :, c:c + chunk] = normed
            packed = jnp.dot(selector, normed, preferred_element_type=F32).astype(BF16)
            for e in range(experts):
                send[m, e, :, c:c + chunk] = packed[e * cap:(e + 1) * cap]
        for order, peer in enumerate(peers):
            dispatch(m, peer, order, me).start()
        recv[m, me] = send[m, own_expert]
        logits = lax.dot_general(nrm[m], router_ref[...], (((1,), (1,)), ((), ())), preferred_element_type=F32)
        scores = jax.nn.sigmoid(logits)
        col = lax.broadcasted_iota(jnp.int32, (tok, 128), 1)
        spread = jnp.zeros((tok, 128), F32)
        for e in range(experts):
            spread = jnp.where(col // (lanes * cap) == e, scores[:, e:e + 1], spread)
        chosen = spread * place_w[m]
        weight = (2.5 * lanes) * chosen / jnp.sum(chosen, axis=1, keepdims=True)
        high = weight.astype(BF16)
        mix[m, 0:tok] = high.astype(F32)
        mix[m, tok:2 * tok] = weight - high.astype(F32)

    def gate_up(m):
        for peer in peers:
            dispatch(m, me, 0, peer).wait_recv()
        groups = recv.shape[1]
        step = 1024

        def body(k, sums):
            ks = pl.ds(pl.multiple_of(k * step, step), step)
            lhs = recv[m, :, :, ks].reshape(groups * cap, step)
            g = sums[0] + jnp.dot(lhs, gate_w[ks, :], preferred_element_type=F32)
            u = sums[1] + jnp.dot(lhs, up_w[ks, :], preferred_element_type=F32)
            return g, u

        zero = jnp.zeros((groups * cap, gate_w.shape[1]), F32)
        g, u = lax.fori_loop(0, width // step, body, (zero, zero))
        act[...] = (g / (1.0 + jnp.exp(-g)) * u).astype(BF16)

    def down(m):
        step = 512

        def body(k, carry):
            ks = pl.ds(pl.multiple_of(k * step, step), step)
            y = jnp.dot(act[...], down_w[:, ks], preferred_element_type=F32).astype(BF16)
            for p in range(n):
                back[m, p, :, ks] = y[p * cap:(p + 1) * cap]
            return carry

        for part in range(2):
            per = half // step
            lax.fori_loop(part * per, (part + 1) * per, body, 0)
            for order, peer in enumerate(peers):
                give_back(m, part, peer, order, me).start()
            cols = pl.ds(part * half, half)
            ret[m, me, :, cols] = back[m, me, :, cols]

    def combine(m):
        for part in range(2):
            for peer in peers:
                give_back(m, part, me, 0, peer).wait_recv()
        weight = mix[m][:, : n * cap].astype(BF16)
        for c in range(0, width, chunk):
            y = jnp.dot(weight, ret[m, :, :, c:c + chunk].reshape(n * cap, chunk), preferred_element_type=F32)
            x = xin[m, :, c:c + chunk].astype(F32)
            out_ref[m, :, c:c + chunk] = (x + (y[:tok] + y[tok:])).astype(BF16)

        @pl.when(section < last)
        def _():
            onward(m).start()

    def step(t, carry):
        @pl.when(t < micro)
        def _():
            start_rows(t)

        @pl.when((t >= 1) & (t <= micro))
        def _():
            @pl.when(t == 1)
            def _():
                weights[0].wait()
                weights[1].wait()
            gate_up(t - 1)

        @pl.when(t >= 2)
        def _():
            combine(t - 2)

        @pl.when((t >= 1) & (t <= micro))
        def _():
            @pl.when(t == 1)
            def _():
                weights[2].wait()
            down(t - 1)

        return carry

    for order, peer in enumerate(peers):
        count_copy(peer, me, order).start()
    counts_in[me] = counts[...]
    lax.fori_loop(0, micro + 2, step, 0)

    for peer in peers:
        count_copy(me, peer, 0).wait_recv()
    hot = hot_ref[0]
    slot_expert = lax.broadcasted_iota(jnp.int32, (1, 128), 1) // (lanes * cap)
    everyone = jnp.sum(counts_in[:, 0, :], axis=0, keepdims=True)
    home = jnp.sum(jnp.where(slot_expert == own_expert, everyone, 0.0), axis=1, keepdims=True)
    extra = jnp.sum(jnp.where(slot_expert == hot // BLOCKS_PER_EXPERT, counts[0:1, :], 0.0), axis=1, keepdims=True)
    share = jnp.where(hot // (BLOCKS_PER_EXPERT // lanes) == me, 1.0, 2.0)
    load_ref[...] = (home * share + extra) / float(lanes * micro * tok * top * BLOCKS_PER_EXPERT)

    for order, peer in enumerate(peers):
        count_copy(peer, me, order).wait_send()

    def drain(m, carry):
        for order, peer in enumerate(peers):
            dispatch(m, peer, order, me).wait_send()
            for part in range(2):
                give_back(m, part, peer, order, me).wait_send()

        @pl.when(section < last)
        def _():
            onward(m).wait_send()

        return carry

    lax.fori_loop(0, micro, drain, 0)


def local(sections, n, rows_in, routes, hot_blocks, gains, router, w_gate, w_up, w_down):
    micro, tok, width = rows_in.shape
    experts, hidden, top = router.shape[2], w_gate.shape[2], routes.shape[3]
    cap = tok // 2
    vmem = pl.BlockSpec(memory_space=pltpu.VMEM)
    hbm = pl.BlockSpec(memory_space=pl.ANY)
    dma = pltpu.SemaphoreType.DMA
    out, load = pl.pallas_call(
        functools.partial(kernel, sections, n, experts, top),
        out_shape=(jax.ShapeDtypeStruct((micro, tok, width), BF16), jax.ShapeDtypeStruct((1, 1), F32)),
        in_specs=[hbm, vmem, pl.BlockSpec(memory_space=pltpu.SMEM), vmem, vmem, hbm, hbm, hbm],
        out_specs=(vmem, vmem),
        scratch_shapes=[
            pltpu.VMEM((width, hidden), BF16),
            pltpu.VMEM((width, hidden), BF16),
            pltpu.VMEM((hidden, width), BF16),
            pltpu.VMEM((micro, tok, width), BF16),
            pltpu.VMEM((micro, experts, cap, width), BF16),
            pltpu.VMEM((micro, n, cap, width), BF16),
            pltpu.VMEM((micro, n, cap, width), BF16),
            pltpu.VMEM((micro, n, cap, width), BF16),
            pltpu.VMEM((micro, tok, width), BF16),
            pltpu.VMEM((micro, tok, 128), F32),
            pltpu.VMEM((micro, experts * cap, tok), BF16),
            pltpu.VMEM((micro, 2 * tok, 128), F32),
            pltpu.VMEM((n * cap, hidden), BF16),
            pltpu.VMEM((8, 128), F32),
            pltpu.VMEM((n, 8, 128), F32),
            dma((3,)), dma((micro,)), dma((micro,)),
            dma((micro, n)), dma((micro, n)), dma((micro, 2, n)), dma((micro, 2, n)), dma((n,)), dma((n,)),
        ],
        compiler_params=pltpu.CompilerParams(collective_id=0, has_side_effects=True, vmem_limit_bytes=56 * 1024 * 1024),
    )(
        rows_in, jnp.swapaxes(routes[0], 1, 2), hot_blocks, gains, router[0].T, w_gate[0], w_up[0], w_down[0],
    )
    return out[None], load


def solution(mesh):
    body = functools.partial(local, mesh.shape["section"], mesh.shape["ep"])
    return jax.shard_map(
        body,
        mesh=mesh,
        in_specs=(
            P(None, "ep", None),
            P("section", None, "ep", None),
            P("section"),
            P("section", None),
            P("section", None, None),
            P("section", None, "ep"),
            P("section", None, "ep"),
            P("section", "ep", None),
        ),
        out_specs=(P("section", None, "ep", None), P("section", "ep")),
        check_vma=False,
    )
```

```python
import functools

import jax
import jax.numpy as jnp
from jax import lax
from jax.experimental import pallas as pl
from jax.experimental.pallas import tpu as pltpu
from jax.sharding import PartitionSpec as P

BLOCKS_PER_EXPERT = 4
PARTS = 4
MESH = pl.DeviceIdType.MESH
F32 = jnp.float32
BF16 = jnp.bfloat16


def flip(index, mask, count):
    result, bit = 0, 1
    while bit < count:
        digit = (index // bit) % 2
        result = result + bit * ((1 - digit) if mask & bit else digit)
        bit *= 2
    return result


def kernel(
    sections, n, experts, top,
    rows_hbm, routes_ref, hot_ref, gains_ref, router_ref, gate_hbm, up_hbm, down_hbm,
    out_ref, load_ref,
    gate_w, up_w, down_w, rows, send, recv, mine, cross_out, cross_in, back, ret, landed,
    gains_all, router_all, place_all, pack_all, act, counts, counts_in,
    weight_sem, entry_sem, in_sem, hop_send, out_send, out_recv, disp_send, disp_recv, cross_send, cross_recv,
    ret_send, ret_recv, count_send, count_recv, param_send, param_recv,
):
    micro, tok, width = landed.shape
    cap = tok // 2
    lanes = n // experts
    hidden = gate_w.shape[1]
    part = width // PARTS
    half = sections // 2
    last = sections - 1
    section = lax.axis_index("section")
    me = lax.axis_index("ep")
    own_expert, lane = me // lanes, me % lanes
    mate = own_expert * lanes + (1 - lane)
    everyone = [flip(me, mask, n) for mask in range(n - 1, -1, -1)]
    peers = everyone[:-1]
    planes = [flip(own_expert, mask, experts) for mask in range(experts - 1, -1, -1)]

    def one(condition):
        return condition.astype(jnp.int32)

    def meeting(layer):
        early, final = one(layer < half), one(layer == last)
        return (early + final) * last, early * layer + final * half + (1 - early - final) * (layer - half)

    weights = [
        pltpu.make_async_copy(source, target, weight_sem.at[i])
        for i, (source, target) in enumerate(((gate_hbm, gate_w), (up_hbm, up_w), (down_hbm, down_w)))
    ]

    def entry(m, place):
        return pltpu.make_async_copy(rows_hbm.at[m], rows.at[place, m], entry_sem.at[m])

    @pl.when(section == 0)
    def _():
        for m in range(micro):
            entry(m, half + 2).start()

    @pl.when(section == last)
    def _():
        for m in range(micro):
            entry(m, 0).start()

    for copy in weights:
        copy.start()

    barrier = pltpu.get_barrier_semaphore()
    for peer in peers:
        pl.semaphore_signal(barrier, inc=1, device_id=(section, peer), device_id_type=MESH)
    partners = 0
    for other in range(sections):
        linked = (section == last) if other <= half else (section < 0)
        if other == last:
            linked = linked | (section <= half)
        if other >= half:
            linked = linked | (section == 0)
        if other == 0:
            linked = linked | (section >= half)
        linked = linked & (section != other)
        partners = partners + one(linked)

        @pl.when(linked)
        def _():
            for peer in everyone:
                pl.semaphore_signal(barrier, inc=1, device_id=(other, peer), device_id_type=MESH)

    held = jnp.zeros((1, 128), F32)
    for m in range(micro):
        slot = lax.broadcasted_iota(jnp.int32, (128, tok), 0)
        expert, rank = slot // cap, slot % cap
        routed = (routes_ref[m, 0:1, :] == expert) | (routes_ref[m, 1:2, :] == expert)
        earlier = (
            lax.broadcasted_iota(jnp.int32, (tok, tok), 0) < lax.broadcasted_iota(jnp.int32, (tok, tok), 1)
        ).astype(BF16)
        taken = jnp.dot(routed.astype(BF16), earlier, preferred_element_type=F32)
        place = jnp.where(routed & (taken == rank.astype(F32)), 1.0, 0.0)
        pack_all[section, m] = place[: experts * cap].astype(BF16)
        place_all[section, m] = place.T
        held = held + jnp.sum(place.T, axis=0, keepdims=True)
    counts[...] = jnp.broadcast_to(held, counts.shape)
    gains_all[section] = gains_ref[...]
    router_all[section] = router_ref[...]

    pl.semaphore_wait(barrier, n - 1 + n * partners)

    def param(i, target, layer, way):
        ref = (gains_all, router_all, place_all, pack_all)[i]
        return pltpu.make_async_remote_copy(
            ref.at[layer], ref.at[layer], param_send.at[way, i], param_recv.at[layer, i],
            device_id=(target, me), device_id_type=MESH,
        )

    def count_copy(peer, source, order):
        return pltpu.make_async_remote_copy(
            counts, counts_in.at[source], count_send.at[order], count_recv.at[source],
            device_id=(section, peer), device_id_type=MESH,
        )

    def seat(source, target):
        other = (source % lanes + lanes - target % lanes) % lanes
        return other * experts + source // lanes

    def dispatch(target, place, m, q, peer, order):
        columns = pl.ds(q * part, part)
        return pltpu.make_async_remote_copy(
            send.at[place, m, peer // lanes, :, columns], recv.at[m, seat(me, peer), :, columns],
            disp_send.at[place, m, q, order], disp_recv.at[m, q, seat(me, peer)],
            device_id=(target, peer), device_id_type=MESH,
        )

    def arrived(m, q, place):
        block = recv.at[m, place, :, pl.ds(q * part, part)]
        return pltpu.make_async_copy(block, block, disp_recv.at[m, q, place])

    def keep(m, q):
        columns = pl.ds(q * part, part)
        return pltpu.make_async_copy(
            send.at[half, m, own_expert, :, columns], recv.at[m, own_expert, :, columns], disp_recv.at[m, q, own_expert]
        )

    def exchange(m, q):
        return pltpu.make_async_remote_copy(
            cross_out.at[m, q], cross_in.at[m, q], cross_send.at[m, q], cross_recv.at[m, q],
            device_id=(section, mate), device_id_type=MESH,
        )

    meet, meet_place = meeting(section)

    def give_back(m, q, plane, order):
        return pltpu.make_async_remote_copy(
            back.at[m, q, plane], ret.at[meet_place, m, q, own_expert], ret_send.at[m, q, order],
            ret_recv.at[meet_place, m, q, own_expert],
            device_id=(meet, plane * lanes + lane), device_id_type=MESH,
        )

    def stay(m, q):
        return pltpu.make_async_copy(
            back.at[m, q, own_expert], ret.at[half, m, q, own_expert], ret_recv.at[half, m, q, own_expert]
        )

    def returned(place, m, q, e):
        block = ret.at[place, m, q, e]
        return pltpu.make_async_copy(block, block, ret_recv.at[place, m, q, e])

    def result(place, m, layer):
        return pltpu.make_async_remote_copy(
            rows.at[place + 1, m], landed.at[m], out_send.at[place, m], out_recv.at[m],
            device_id=(layer, me), device_id_type=MESH,
        )

    def moved(place, m, target, there):
        return pltpu.make_async_remote_copy(
            rows.at[place + 1, m], rows.at[there, m], hop_send.at[m], in_sem.at[m],
            device_id=(target, me), device_id_type=MESH,
        )

    def came(m, place):
        return pltpu.make_async_copy(rows.at[place, m], rows.at[place, m], in_sem.at[m])

    def send_rows(target, place, m, source, square, gain, selector):
        scale = lax.rsqrt(square / width + 1e-06)
        for q in range(PARTS):
            columns = slice(q * part, (q + 1) * part)
            normed = (rows[source, m, :, columns].astype(F32) * scale * gain[:, columns]).astype(BF16)
            packed = jnp.dot(selector, normed, preferred_element_type=F32).astype(BF16)
            for e in range(experts):
                send[place, m, e, :, columns] = packed[e * cap:(e + 1) * cap]
            for order, peer in enumerate(peers):
                dispatch(target, place, m, q, peer, order).start()
            if target is section:
                keep(m, q).start()
            else:
                dispatch(target, place, m, q, me, n - 1).start()

    def first_rows(m):
        entry(m, half + 2).wait()
        x = rows[half + 2, m].astype(F32)
        send_rows(section, half, m, half + 2, jnp.sum(x * x, axis=-1, keepdims=True), gains_ref, pack_all[section, m])

    def gate_up(m):
        g = jnp.zeros((n * cap, hidden), F32)
        u = jnp.zeros((n * cap, hidden), F32)
        for q in range(PARTS):
            for place in range(n):
                arrived(m, q, place).wait()
            columns = slice(q * part, (q + 1) * part)
            lhs = recv[m, :, :, columns].reshape(n * cap, part)
            g = g + jnp.dot(lhs, gate_w[columns, :], preferred_element_type=F32)
            u = u + jnp.dot(lhs, up_w[columns, :], preferred_element_type=F32)
        act[...] = (g / (1.0 + jnp.exp(-g)) * u).astype(BF16)

    def down(m):
        for q in range(PARTS):
            columns = slice(q * part, (q + 1) * part)
            y = jnp.dot(act[...], down_w[:, columns], preferred_element_type=F32)
            mine[q] = y[: experts * cap]
            for p in range(experts):
                cross_out[m, q, p] = y[(experts + p) * cap:(experts + p + 1) * cap].astype(BF16)
            exchange(m, q).start()

    def pair(m):
        for q in range(PARTS):
            exchange(m, q).wait_recv()
            both = (mine[q] + cross_in[m, q].reshape(experts * cap, part).astype(F32)).astype(BF16)
            for p in range(experts):
                back[m, q, p] = both[p * cap:(p + 1) * cap]
            for order, plane in enumerate(planes[:-1]):
                give_back(m, q, plane, order).start()

            @pl.when(section == last)
            def _():
                stay(m, q).start()

            @pl.when(section < last)
            def _():
                give_back(m, q, own_expert, experts - 1).start()

    def gates(layer, source, m):
        x = rows[source, m].astype(F32)
        scale = lax.rsqrt(jnp.mean(x * x, axis=-1, keepdims=True) + 1e-06)
        normed = (x * scale * gains_all[layer]).astype(BF16)
        logits = lax.dot_general(normed, router_all[layer], (((1,), (1,)), ((), ())), preferred_element_type=F32)
        scores = jax.nn.sigmoid(logits)
        col = lax.broadcasted_iota(jnp.int32, (tok, 128), 1)
        spread = jnp.zeros((tok, 128), F32)
        for e in range(experts):
            spread = jnp.where(col // cap == e, scores[:, e:e + 1], spread)
        chosen = spread * place_all[layer, m]
        weight = 2.5 * chosen / jnp.sum(chosen, axis=1, keepdims=True)
        high = weight.astype(BF16).astype(F32)
        return jnp.concatenate([high, weight - high], axis=0)[:, : experts * cap].astype(BF16)

    def combine(place, source, m, weight, final):
        square = jnp.zeros((tok, 1), F32)
        for q in range(PARTS):
            for e in range(experts):
                returned(place, m, q, e).wait()
            columns = slice(q * part, (q + 1) * part)
            y = jnp.dot(weight, ret[place, m, q].reshape(experts * cap, part), preferred_element_type=F32)
            x = rows[source, m, :, columns].astype(F32)
            z = (x + (y[:tok] + y[tok:])).astype(BF16)
            if final:
                out_ref[m, :, columns] = z
            else:
                rows[source + 1, m, :, columns] = z
                z = z.astype(F32)
                square = square + jnp.sum(z * z, axis=-1, keepdims=True)
        return square

    def finish(layer, m):
        _, place = meeting(layer)

        @pl.when(layer == 0)
        def _():
            entry(m, 0).wait()

        @pl.when(layer == half)
        def _():
            came(m, 0).wait()

        weight = gates(layer, place, m)
        square = combine(place, place, m, weight, False)
        send_rows(layer + 1, place, m, place + 1, square, gains_all[layer + 1], pack_all[layer + 1, m])

        @pl.when(layer == half - 1)
        def _():
            moved(place, m, 0, 0).start()

        @pl.when(layer == last - 1)
        def _():
            moved(place, m, last, half + 1).start()

        result(place, m, layer).start()

    def final(m):
        came(m, half + 1).wait()
        combine(half, half + 1, m, gates(last, half + 1, m), True)

    @pl.when(section == 0)
    def _():
        first_rows(0)

    @pl.when((section <= half) & (section < last))
    def _():
        for i in range(4):
            param(i, last, section, 0).start()

    @pl.when(section >= half)
    def _():
        for i in range(4):
            param(i, 0, section, 1).start()

    @pl.when(section == 0)
    def _():
        first_rows(1)

    for order, peer in enumerate(peers):
        count_copy(peer, me, order).start()
    counts_in[me] = counts[...]

    def wave(begin, count):
        def turn(k, carry):
            def layer_turn(i, carry):
                m = k - 2 * i

                @pl.when((m >= 0) & (m < micro))
                def _():
                    finish(begin + i, m)

                return carry

            return lax.fori_loop(0, count, layer_turn, carry)

        lax.fori_loop(0, micro + 2 * (count - 1), turn, 0)

    @pl.when(section == last)
    def _():
        for layer in range(half + 1):
            for i in range(4):
                param(i, 0, layer, 0).wait_recv()
        wave(0, half)

    weights[0].wait()
    weights[1].wait()

    def step(m, carry):
        gate_up(m)

        @pl.when(m == 0)
        def _():
            weights[2].wait()

        down(m)

        @pl.when((section == 0) & (m < micro - 2))
        def _():
            first_rows(m + 2)

        pair(m)

        @pl.when((section == last) & (m > 0))
        def _():
            final(m - 1)

        return carry

    lax.fori_loop(0, micro, step, 0)

    @pl.when(section == last)
    def _():
        final(micro - 1)

    @pl.when(section == 0)
    def _():
        for layer in range(half, sections):
            for i in range(4):
                param(i, 0, layer, 0).wait_recv()
        wave(half, half - 1)

    for peer in peers:
        count_copy(me, peer, 0).wait_recv()
    hot = hot_ref[...]
    slot_expert = lax.broadcasted_iota(jnp.int32, (1, 128), 1) // cap
    total = jnp.sum(counts_in[:, 0, :], axis=0, keepdims=True)
    home = jnp.sum(jnp.where(slot_expert == own_expert, total, 0.0), axis=1, keepdims=True)
    extra = jnp.sum(jnp.where(slot_expert == hot // BLOCKS_PER_EXPERT, counts[0:1, :], 0.0), axis=1, keepdims=True)
    share = jnp.where(hot // (BLOCKS_PER_EXPERT // lanes) == me, 1.0, 2.0)
    load_ref[...] = (home * share + extra) / float(micro * tok * top * BLOCKS_PER_EXPERT)

    @pl.when(section < last)
    def _():
        def take(m, carry):
            pltpu.make_async_copy(landed.at[m], landed.at[m], out_recv.at[m]).wait()
            out_ref[m] = landed[m]
            return carry

        lax.fori_loop(0, micro, take, 0)

    for order, peer in enumerate(peers):
        count_copy(peer, me, order).wait_send()

    @pl.when((section <= half) & (section < last))
    def _():
        for i in range(4):
            param(i, last, section, 0).wait_send()

    @pl.when(section >= half)
    def _():
        for i in range(4):
            param(i, 0, section, 1).wait_send()

    def drain(m, carry):
        for q in range(PARTS):
            exchange(m, q).wait_send()
            for order, plane in enumerate(planes[:-1]):
                give_back(m, q, plane, order).wait_send()

            @pl.when(section < last)
            def _():
                give_back(m, q, own_expert, experts - 1).wait_send()

            @pl.when(section == 0)
            def _():
                for order, peer in enumerate(peers):
                    dispatch(section, half, m, q, peer, order).wait_send()

        def drain_layer(place, carry):
            for q in range(PARTS):
                for order, peer in enumerate(everyone):
                    dispatch(section, place, m, q, peer, order).wait_send()
            result(place, m, section).wait_send()
            return carry

        @pl.when(section == last)
        def _():
            lax.fori_loop(0, half, drain_layer, 0)
            moved(0, m, 0, 0).wait_send()

        @pl.when(section == 0)
        def _():
            lax.fori_loop(0, half - 1, drain_layer, 0)
            moved(0, m, 0, 0).wait_send()

        return carry

    lax.fori_loop(0, micro, drain, 0)


def local(sections, n, rows_in, routes, hot_blocks, gains, router, w_gate, w_up, w_down):
    micro, tok, width = rows_in.shape
    experts, hidden, top = router.shape[2], w_gate.shape[2], routes.shape[3]
    cap, half, part = tok // 2, sections // 2, width // PARTS
    vmem = pl.BlockSpec(memory_space=pltpu.VMEM)
    hbm = pl.BlockSpec(memory_space=pl.ANY)
    dma = pltpu.SemaphoreType.DMA
    out, load = pl.pallas_call(
        functools.partial(kernel, sections, n, experts, top),
        out_shape=(jax.ShapeDtypeStruct((micro, tok, width), BF16), jax.ShapeDtypeStruct((1, 1), F32)),
        in_specs=[hbm, vmem, vmem, vmem, vmem, hbm, hbm, hbm],
        out_specs=(vmem, vmem),
        scratch_shapes=[
            pltpu.VMEM((width, hidden), BF16),
            pltpu.VMEM((width, hidden), BF16),
            pltpu.VMEM((hidden, width), BF16),
            pltpu.VMEM((half + 3, micro, tok, width), BF16),
            pltpu.VMEM((half + 1, micro, experts, cap, width), BF16),
            pltpu.VMEM((micro, n, cap, width), BF16),
            pltpu.VMEM((PARTS, experts * cap, part), F32),
            pltpu.VMEM((micro, PARTS, experts, cap, part), BF16),
            pltpu.VMEM((micro, PARTS, experts, cap, part), BF16),
            pltpu.VMEM((micro, PARTS, experts, cap, part), BF16),
            pltpu.VMEM((half + 1, micro, PARTS, experts, cap, part), BF16),
            pltpu.VMEM((micro, tok, width), BF16),
            pltpu.VMEM((sections, 1, width), F32),
            pltpu.VMEM((sections, experts, width), BF16),
            pltpu.VMEM((sections, micro, tok, 128), F32),
            pltpu.VMEM((sections, micro, experts * cap, tok), BF16),
            pltpu.VMEM((n * cap, hidden), BF16),
            pltpu.VMEM((8, 128), F32),
            pltpu.VMEM((n, 8, 128), F32),
            dma((3,)), dma((micro,)), dma((micro,)), dma((micro,)), dma((half, micro)), dma((micro,)),
            dma((half + 1, micro, PARTS, n)), dma((micro, PARTS, n)), dma((micro, PARTS)), dma((micro, PARTS)),
            dma((micro, PARTS, experts)), dma((half + 1, micro, PARTS, experts)), dma((n,)), dma((n,)),
            dma((2, 4)), dma((sections, 4)),
        ],
        compiler_params=pltpu.CompilerParams(collective_id=0, has_side_effects=True, vmem_limit_bytes=60 * 1024 * 1024),
    )(
        rows_in, jnp.swapaxes(routes[0], 1, 2), hot_blocks.reshape(1, 1), gains, router[0].T, w_gate[0], w_up[0], w_down[0],
    )
    return out[None], load


def solution(mesh):
    body = functools.partial(local, mesh.shape["section"], mesh.shape["ep"])
    return jax.shard_map(
        body,
        mesh=mesh,
        in_specs=(
            P(None, "ep", None),
            P("section", None, "ep", None),
            P("section"),
            P("section", None),
            P("section", None, None),
            P("section", None, "ep"),
            P("section", None, "ep"),
            P("section", "ep", None),
        ),
        out_specs=(P("section", None, "ep", None), P("section", "ep")),
        check_vma=False,
    )
```

```python
import functools

import jax
import jax.numpy as jnp
from jax import lax
from jax.experimental import pallas as pl
from jax.experimental.pallas import tpu as pltpu
from jax.sharding import PartitionSpec as P

BLOCKS_PER_EXPERT = 4
PARTS = 4
START, ENTRY, SUM = range(3)
FIRST = 1
HERE = 2
MESH = pl.DeviceIdType.MESH
F32 = jnp.float32
BF16 = jnp.bfloat16


def flip(index, mask, count):
    result, bit = 0, 1
    while bit < count:
        digit = (index // bit) % 2
        result = result + bit * ((1 - digit) if mask & bit else digit)
        bit *= 2
    return result


def kernel(
    sections, n, experts, top,
    rows_hbm, routes_ref, hot_ref, gains_ref, router_ref, gate_hbm, up_hbm, down_hbm,
    out_ref, load_ref,
    gate_w, up_w, down_w, rows, send, recv, mine, cross_out, cross_in, back, ret,
    gains_all, router_all, place_all, pack_all, act, counts, counts_in,
    weight_sem, entry_sem, out_send, out_recv, disp_send, disp_recv, cross_send, cross_recv,
    ret_send, ret_recv, count_send, count_recv, param_send, param_recv,
):
    _, micro, tok, width = rows.shape
    cap = tok // 2
    lanes = n // experts
    hidden = gate_w.shape[1]
    part = width // PARTS
    last = sections - 1
    section = lax.axis_index("section")
    me = lax.axis_index("ep")
    own_expert, lane = me // lanes, me % lanes
    mate = own_expert * lanes + (1 - lane)
    everyone = [flip(me, mask, n) for mask in range(n - 1, -1, -1)]
    peers = everyone[:-1]
    planes = [flip(own_expert, mask, experts) for mask in range(experts - 1, -1, -1)]

    def one(condition):
        return condition.astype(jnp.int32)

    def meeting(layer):
        edge = one(layer == 0) + one(layer == last)
        return edge * last + (1 - edge) * (layer - 1), one(layer == last)

    weights = [
        pltpu.make_async_copy(source, target, weight_sem.at[i])
        for i, (source, target) in enumerate(((gate_hbm, gate_w), (up_hbm, up_w), (down_hbm, down_w)))
    ]

    def entry(m):
        return pltpu.make_async_copy(rows_hbm.at[m], rows.at[ENTRY, m], entry_sem.at[m])

    @pl.when(section == 0)
    def _():
        for m in range(HERE):
            entry(m).start()

    @pl.when(section == last)
    def _():
        for m in range(micro):
            entry(m).start()

    for copy in weights:
        copy.start()

    barrier = pltpu.get_barrier_semaphore()
    for peer in peers:
        pl.semaphore_signal(barrier, inc=1, device_id=(section, peer), device_id_type=MESH)
    partners = 0
    for other in range(sections):
        linked = (section == other - 2) | (section == other + 2)
        if other < last:
            linked = linked | (section == other - 1)
        if other < last - 1:
            linked = linked | (section == other + 1)
        if other < 2:
            linked = linked | (section == last)
        if other == last:
            linked = linked | (section < 2)
        linked = linked & (section != other)
        partners = partners + one(linked)

        @pl.when(linked)
        def _():
            for peer in everyone:
                pl.semaphore_signal(barrier, inc=1, device_id=(other, peer), device_id_type=MESH)

    def placement(m, count):
        slot = lax.broadcasted_iota(jnp.int32, (count, tok), 0)
        expert, rank = slot // cap, slot % cap
        routed = (routes_ref[m, 0:1, :] == expert) | (routes_ref[m, 1:2, :] == expert)
        earlier = (
            lax.broadcasted_iota(jnp.int32, (tok, tok), 0) < lax.broadcasted_iota(jnp.int32, (tok, tok), 1)
        ).astype(BF16)
        taken = jnp.dot(routed.astype(BF16), earlier, preferred_element_type=F32)
        return jnp.where(routed & (taken == rank.astype(F32)), 1.0, 0.0)

    for m in range(micro):
        pack_all[section, m] = placement(m, experts * cap).astype(BF16)

    pl.semaphore_wait(barrier, n - 1 + n * partners)

    def param(i, target, layer, way):
        ref = (gains_all, router_all, place_all, pack_all)[i]
        return pltpu.make_async_remote_copy(
            ref.at[layer], ref.at[layer], param_send.at[way, i], param_recv.at[layer, i],
            device_id=(target, me), device_id_type=MESH,
        )

    def count_copy(peer, source, order):
        return pltpu.make_async_remote_copy(
            counts, counts_in.at[source], count_send.at[order], count_recv.at[source],
            device_id=(section, peer), device_id_type=MESH,
        )

    def seat(source, target):
        other = (source % lanes + lanes - target % lanes) % lanes
        return other * experts + source // lanes

    def dispatch(target, place, m, q, peer):
        columns = pl.ds(q * part, part)
        return pltpu.make_async_remote_copy(
            send.at[place, m, peer // lanes, :, columns], recv.at[m, seat(me, peer), :, columns],
            disp_send.at[place, m, q], disp_recv.at[m, q, seat(me, peer)],
            device_id=(target, peer), device_id_type=MESH,
        )

    def arrived(m, q, place):
        block = recv.at[m, place, :, pl.ds(q * part, part)]
        return pltpu.make_async_copy(block, block, disp_recv.at[m, q, place])

    def keep(m, q):
        columns = pl.ds(q * part, part)
        return pltpu.make_async_copy(
            send.at[FIRST, m, own_expert, :, columns], recv.at[m, own_expert, :, columns], disp_recv.at[m, q, own_expert]
        )

    def exchange(m, q):
        return pltpu.make_async_remote_copy(
            cross_out.at[m, q], cross_in.at[m, q], cross_send.at[m], cross_recv.at[m, q],
            device_id=(section, mate), device_id_type=MESH,
        )

    meet, meet_place = meeting(section)

    def give_back(m, q, plane):
        return pltpu.make_async_remote_copy(
            back.at[m, q, plane], ret.at[meet_place, m, q, own_expert], ret_send.at[m],
            ret_recv.at[meet_place, m, q, own_expert],
            device_id=(meet, plane * lanes + lane), device_id_type=MESH,
        )

    def stay(m, q):
        return pltpu.make_async_copy(
            back.at[m, q, own_expert], ret.at[1, m, q, own_expert], ret_recv.at[1, m, q, own_expert]
        )

    def returned(place, m, q, e):
        block = ret.at[place, m, q, e]
        return pltpu.make_async_copy(block, block, ret_recv.at[place, m, q, e])

    def result(m, target, i):
        return pltpu.make_async_remote_copy(
            rows.at[SUM, m], rows.at[START, m], out_send.at[i, m], out_recv.at[m], device_id=(target, me), device_id_type=MESH,
        )

    def landed(m):
        return pltpu.make_async_copy(rows.at[START, m], rows.at[START, m], out_recv.at[m])

    def gone(place, m, q, count=n):
        block = recv.at[m, pl.ds(0, count), :, pl.ds(q * part, part)]
        pltpu.make_async_copy(block, block, disp_send.at[place, m, q]).wait()

    def send_rows(target, place, m, source, square, gain, selector, own=False):
        scale = lax.rsqrt(square / width + 1e-06)
        for q in range(PARTS):
            if not place:
                @pl.when(m > 0)
                def _():
                    for r in ((0, 1) if q == 0 else (q + 1,) if q < PARTS - 1 else ()):
                        gone(place, m - 1, r)

            columns = slice(q * part, (q + 1) * part)
            normed = (rows[source, m, :, columns].astype(F32) * scale * gain[:, columns]).astype(BF16)
            packed = jnp.dot(selector, normed, preferred_element_type=F32).astype(BF16)
            for e in range(experts):
                send[place, m, e, :, columns] = packed[e * cap:(e + 1) * cap]
            for peer in peers:
                dispatch(target, place, m, q, peer).start()
            if own:
                keep(m, q).start()
            else:
                dispatch(target, place, m, q, me).start()

    def first_rows(m, gain, selector, own):
        entry(m).wait()
        x = rows[ENTRY, m].astype(F32)
        send_rows(0, FIRST, m, ENTRY, jnp.sum(x * x, axis=-1, keepdims=True), gain, selector, own)

    def gate_up(m):
        g = jnp.zeros((n * cap, hidden), F32)
        u = jnp.zeros((n * cap, hidden), F32)
        for q in range(PARTS):
            for place in range(n):
                arrived(m, q, place).wait()
            if q == 1:
                @pl.when((section == 0) & (m < HERE - 1))
                def _():
                    first_rows(m + 1, gains_ref, pack_all[0, m + 1], True)
            columns = slice(q * part, (q + 1) * part)
            lhs = recv[m, :, :, columns].reshape(n * cap, part)
            g = g + jnp.dot(lhs, gate_w[columns, :], preferred_element_type=F32)
            u = u + jnp.dot(lhs, up_w[columns, :], preferred_element_type=F32)
        act[...] = (g / (1.0 + jnp.exp(-g)) * u).astype(BF16)

    def down(m):
        for q in range(PARTS):
            columns = slice(q * part, (q + 1) * part)
            y = jnp.dot(act[...], down_w[:, columns], preferred_element_type=F32)
            mine[q] = y[: experts * cap]
            for p in range(experts):
                cross_out[m, q, p] = y[(experts + p) * cap:(experts + p + 1) * cap].astype(BF16)
            exchange(m, q).start()

    def pair(m):
        for q in range(PARTS):
            exchange(m, q).wait_recv()
            both = (mine[q] + cross_in[m, q].reshape(experts * cap, part).astype(F32)).astype(BF16)
            for p in range(experts):
                back[m, q, p] = both[p * cap:(p + 1) * cap]
            for plane in planes[:-1]:
                give_back(m, q, plane).start()

            @pl.when(section == last)
            def _():
                stay(m, q).start()

            @pl.when(section < last)
            def _():
                give_back(m, q, own_expert).start()

    def gates(layer, source, m):
        x = rows[source, m].astype(F32)
        scale = lax.rsqrt(jnp.mean(x * x, axis=-1, keepdims=True) + 1e-06)
        normed = (x * scale * gains_all[layer]).astype(BF16)
        logits = lax.dot_general(normed, router_all[layer], (((1,), (1,)), ((), ())), preferred_element_type=F32)
        scores = jax.nn.sigmoid(logits)
        col = lax.broadcasted_iota(jnp.int32, (tok, 128), 1)
        spread = jnp.zeros((tok, 128), F32)
        for e in range(experts):
            spread = jnp.where(col // cap == e, scores[:, e:e + 1], spread)
        chosen = spread * place_all[layer, m]
        weight = 2.5 * chosen / jnp.sum(chosen, axis=1, keepdims=True)
        high = weight.astype(BF16).astype(F32)
        return jnp.concatenate([high, weight - high], axis=0)[:, : experts * cap].astype(BF16)

    def combine(place, source, m, weight, final):
        square = jnp.zeros((tok, 1), F32)
        for q in range(PARTS):
            for e in range(experts):
                returned(place, m, q, e).wait()
            columns = slice(q * part, (q + 1) * part)
            y = jnp.dot(weight, ret[place, m, q].reshape(experts * cap, part), preferred_element_type=F32)
            x = rows[source, m, :, columns].astype(F32)
            z = (x + (y[:tok] + y[tok:])).astype(BF16)
            if final:
                out_ref[m, :, columns] = z
            else:
                rows[SUM, m, :, columns] = z
                z = z.astype(F32)
                square = square + jnp.sum(z * z, axis=-1, keepdims=True)
        return square

    def finish(layer, source, m):
        weight = gates(layer, source, m)
        square = combine(0, source, m, weight, False)
        send_rows(layer + 1, 0, m, SUM, square, gains_all[layer + 1], pack_all[layer + 1, m])
        result(m, layer, 0).start()

        @pl.when(layer == last - 1)
        def _():
            result(m, last, 1).start()

    def final(m):
        landed(m).wait()
        combine(1, START, m, gates(last, START, m), True)

    def left(ref, semaphore):
        pltpu.make_async_copy(ref, ref, semaphore).wait()

    def sent(m):
        left(cross_out.at[m], cross_send.at[m])

        @pl.when(section < last)
        def _():
            left(back.at[m], ret_send.at[m])

        @pl.when(section == last)
        def _():
            left(recv.at[m, pl.ds(0, experts - 1)], ret_send.at[m])

    def load():
        for peer in peers:
            count_copy(me, peer, 0).wait_recv()
        hot = hot_ref[...]
        slot_expert = lax.broadcasted_iota(jnp.int32, (1, 128), 1) // cap
        total = jnp.sum(counts_in[:, 0, :], axis=0, keepdims=True)
        home = jnp.sum(jnp.where(slot_expert == own_expert, total, 0.0), axis=1, keepdims=True)
        extra = jnp.sum(jnp.where(slot_expert == hot // BLOCKS_PER_EXPERT, counts[0:1, :], 0.0), axis=1, keepdims=True)
        share = jnp.where(hot // (BLOCKS_PER_EXPERT // lanes) == me, 1.0, 2.0)
        load_ref[...] = (home * share + extra) / float(micro * tok * top * BLOCKS_PER_EXPERT)
        for order, peer in enumerate(peers):
            count_copy(peer, me, order).wait_send()

    @pl.when(section == 0)
    def _():
        first_rows(0, gains_ref, pack_all[0, 0], True)

    held = jnp.zeros((1, 128), F32)
    for m in range(micro):
        place = placement(m, 128).T
        place_all[section, m] = place
        held = held + jnp.sum(place, axis=0, keepdims=True)
    counts[...] = jnp.broadcast_to(held, counts.shape)
    gains_all[section] = gains_ref[...]
    router_all[section] = router_ref[...]

    def params(act_on):
        @pl.when(section < 2)
        def _():
            for i in range(4):
                act_on(param(i, last, section, 0))

        @pl.when(section >= 2)
        def _():
            for i in range(4):
                act_on(param(i, section - 2, section, 0))

        @pl.when((section >= 1) & (section < last))
        def _():
            for i in range(4):
                act_on(param(i, section - 1, section, 1))

    params(lambda copy: copy.start())

    for order, peer in enumerate(peers):
        count_copy(peer, me, order).start()
    counts_in[me] = counts[...]

    @pl.when(section == last)
    def _():
        for layer in range(2):
            for i in range(4):
                param(i, 0, layer, 0).wait_recv()

        def begin(m, carry):
            first_rows(m, gains_all[0], pack_all[0, m], False)
            return carry

        lax.fori_loop(HERE, micro, begin, 0)
        for m in range(HERE):
            entry(m).wait()

        def turn(m, carry):
            finish(0, ENTRY, m)
            return carry

        lax.fori_loop(0, micro, turn, 0)

    weights[0].wait()
    weights[1].wait()

    gate_up(0)
    eager = section >= 0

    def step(m, carry):
        @pl.when(m == 0)
        def _():
            weights[2].wait()

        down(m)

        @pl.when(m == 0)
        def _():
            load()

        @pl.when((m < micro - 1) & eager)
        def _():
            gate_up(m + 1)

        pair(m)

        @pl.when((m < micro - 1) & jnp.logical_not(eager))
        def _():
            gate_up(m + 1)

        @pl.when(m > 0)
        def _():
            sent(m - 1)

            @pl.when(section == last)
            def _():
                final(m - 1)

        return carry

    lax.fori_loop(0, micro, step, 0)

    @pl.when(section == last)
    def _():
        final(micro - 1)

    @pl.when(section < last - 1)
    def _():
        for i in range(4):
            param(i, 0, section + 1, 0).wait_recv()
            param(i, 0, section + 2, 0).wait_recv()

        def turn(m, carry):
            landed(m).wait()
            out_ref[m] = rows[START, m]
            finish(section + 1, START, m)
            return carry

        lax.fori_loop(0, micro, turn, 0)

    @pl.when(section == last - 1)
    def _():
        def take(m, carry):
            landed(m).wait()
            out_ref[m] = rows[START, m]
            return carry

        lax.fori_loop(0, micro, take, 0)

    sent(micro - 1)
    params(lambda copy: copy.wait_send())

    @pl.when(section != last - 1)
    def _():
        for q in range(PARTS):
            gone(0, micro - 1, q)

    def drain(m, carry):
        @pl.when(section != last - 1)
        def _():
            result(m, section, 0).wait_send()

        @pl.when(section == last - 2)
        def _():
            result(m, section, 1).wait_send()

        @pl.when((section == 0) & (m < HERE))
        def _():
            for q in range(PARTS):
                gone(FIRST, m, q, n - 1)

        @pl.when((section == last) & (m >= HERE))
        def _():
            for q in range(PARTS):
                gone(FIRST, m, q)

        return carry

    lax.fori_loop(0, micro, drain, 0)


def local(sections, n, rows_in, routes, hot_blocks, gains, router, w_gate, w_up, w_down):
    micro, tok, width = rows_in.shape
    experts, hidden, top = router.shape[2], w_gate.shape[2], routes.shape[3]
    cap, part = tok // 2, width // PARTS
    vmem = pl.BlockSpec(memory_space=pltpu.VMEM)
    hbm = pl.BlockSpec(memory_space=pl.ANY)
    dma = pltpu.SemaphoreType.DMA
    out, load = pl.pallas_call(
        functools.partial(kernel, sections, n, experts, top),
        out_shape=(jax.ShapeDtypeStruct((micro, tok, width), BF16), jax.ShapeDtypeStruct((1, 1), F32)),
        in_specs=[hbm, vmem, vmem, vmem, vmem, hbm, hbm, hbm],
        out_specs=(vmem, vmem),
        scratch_shapes=[
            pltpu.VMEM((width, hidden), BF16),
            pltpu.VMEM((width, hidden), BF16),
            pltpu.VMEM((hidden, width), BF16),
            pltpu.VMEM((3, micro, tok, width), BF16),
            pltpu.VMEM((2, micro, experts, cap, width), BF16),
            pltpu.VMEM((micro, n, cap, width), BF16),
            pltpu.VMEM((PARTS, experts * cap, part), F32),
            pltpu.VMEM((micro, PARTS, experts, cap, part), BF16),
            pltpu.VMEM((micro, PARTS, experts, cap, part), BF16),
            pltpu.VMEM((micro, PARTS, experts, cap, part), BF16),
            pltpu.VMEM((2, micro, PARTS, experts, cap, part), BF16),
            pltpu.VMEM((sections, 1, width), F32),
            pltpu.VMEM((sections, experts, width), BF16),
            pltpu.VMEM((sections, micro, tok, 128), F32),
            pltpu.VMEM((sections, micro, experts * cap, tok), BF16),
            pltpu.VMEM((n * cap, hidden), BF16),
            pltpu.VMEM((8, 128), F32),
            pltpu.VMEM((n, 8, 128), F32),
            dma((3,)), dma((micro,)), dma((2, micro)), dma((micro,)),
            dma((2, micro, PARTS)), dma((micro, PARTS, n)), dma((micro,)), dma((micro, PARTS)),
            dma((micro,)), dma((2, micro, PARTS, experts)), dma((n,)), dma((n,)),
            dma((2, 4)), dma((sections, 4)),
        ],
        compiler_params=pltpu.CompilerParams(collective_id=0, has_side_effects=True, vmem_limit_bytes=60 * 1024 * 1024),
    )(
        rows_in, jnp.swapaxes(routes[0], 1, 2), hot_blocks.reshape(1, 1), gains, router[0].T, w_gate[0], w_up[0], w_down[0],
    )
    return out[None], load


def solution(mesh):
    body = functools.partial(local, mesh.shape["section"], mesh.shape["ep"])
    return jax.shard_map(
        body,
        mesh=mesh,
        in_specs=(
            P(None, "ep", None),
            P("section", None, "ep", None),
            P("section"),
            P("section", None),
            P("section", None, None),
            P("section", None, "ep"),
            P("section", None, "ep"),
            P("section", "ep", None),
        ),
        out_specs=(P("section", None, "ep", None), P("section", "ep")),
        check_vma=False,
    )
```

```python
import functools

import jax
import jax.numpy as jnp
from jax import lax
from jax.experimental import pallas as pl
from jax.experimental.pallas import tpu as pltpu
from jax.sharding import PartitionSpec as P

BLOCKS_PER_EXPERT = 4
PARTS = 4
START, ENTRY, SUM, EXTRA = range(4)
FIRST, ASIDE = 1, 2
HERE = 2
MESH = pl.DeviceIdType.MESH
F32 = jnp.float32
BF16 = jnp.bfloat16


def flip(index, mask, count):
    result, bit = 0, 1
    while bit < count:
        digit = (index // bit) % 2
        result = result + bit * ((1 - digit) if mask & bit else digit)
        bit *= 2
    return result


def kernel(
    sections, n, experts, top,
    rows_hbm, routes_ref, hot_ref, gains_ref, router_ref, gate_hbm, up_hbm, down_hbm,
    out_ref, load_ref,
    gate_w, up_w, down_w, rows, send, recv, mine, cross_out, cross_in, back, ret,
    gains_all, router_all, place_all, pack_all, act, counts, counts_in,
    weight_sem, entry_sem, out_send, out_recv, disp_send, disp_recv, cross_send, cross_recv,
    ret_send, ret_recv, count_send, count_recv, param_send, param_recv,
):
    _, micro, tok, width = rows.shape
    cap = tok // 2
    lanes = n // experts
    hidden = gate_w.shape[1]
    part = width // PARTS
    last = sections - 1
    section = lax.axis_index("section")
    me = lax.axis_index("ep")
    own_expert, lane = me // lanes, me % lanes
    mate = own_expert * lanes + (1 - lane)
    everyone = [flip(me, mask, n) for mask in range(n - 1, -1, -1)]
    peers = everyone[:-1]
    planes = [flip(own_expert, mask, experts) for mask in range(experts - 1, -1, -1)]

    def one(condition):
        return condition.astype(jnp.int32)

    def meeting(layer):
        edge = one(layer == 0) + one(layer == last)
        return edge * last + (1 - edge) * (layer - 1), one(layer == last)

    weights = [
        pltpu.make_async_copy(source, target, weight_sem.at[i])
        for i, (source, target) in enumerate(((gate_hbm, gate_w), (up_hbm, up_w), (down_hbm, down_w)))
    ]

    def entry(m):
        return pltpu.make_async_copy(rows_hbm.at[m], rows.at[ENTRY, m], entry_sem.at[m])

    @pl.when(section == 0)
    def _():
        for m in range(HERE):
            entry(m).start()

    @pl.when(section == last)
    def _():
        for m in range(micro):
            entry(m).start()

    for copy in weights:
        copy.start()

    barrier = pltpu.get_barrier_semaphore()
    for peer in peers:
        pl.semaphore_signal(barrier, inc=1, device_id=(section, peer), device_id_type=MESH)
    partners = 0
    for other in range(sections):
        linked = (section == other - 2) | (section == other + 2)
        if other < last:
            linked = linked | (section == other - 1)
        if other < last - 1:
            linked = linked | (section == other + 1)
        if other < 3:
            linked = linked | (section == last)
        if other == last:
            linked = linked | (section < 3)
        linked = linked & (section != other)
        partners = partners + one(linked)

        @pl.when(linked)
        def _():
            for peer in everyone:
                pl.semaphore_signal(barrier, inc=1, device_id=(other, peer), device_id_type=MESH)

    def placement(m, count):
        slot = lax.broadcasted_iota(jnp.int32, (count, tok), 0)
        expert, rank = slot // cap, slot % cap
        routed = (routes_ref[m, 0:1, :] == expert) | (routes_ref[m, 1:2, :] == expert)
        earlier = (
            lax.broadcasted_iota(jnp.int32, (tok, tok), 0) < lax.broadcasted_iota(jnp.int32, (tok, tok), 1)
        ).astype(BF16)
        taken = jnp.dot(routed.astype(BF16), earlier, preferred_element_type=F32)
        return jnp.where(routed & (taken == rank.astype(F32)), 1.0, 0.0)

    for m in range(micro):
        pack_all[section, m] = placement(m, experts * cap).astype(BF16)

    pl.semaphore_wait(barrier, n - 1 + n * partners)

    def param(i, target, layer, way):
        ref = (gains_all, router_all, place_all, pack_all)[i]
        return pltpu.make_async_remote_copy(
            ref.at[layer], ref.at[layer], param_send.at[way, i], param_recv.at[layer, i],
            device_id=(target, me), device_id_type=MESH,
        )

    def count_copy(peer, source, order):
        return pltpu.make_async_remote_copy(
            counts, counts_in.at[source], count_send.at[order], count_recv.at[source],
            device_id=(section, peer), device_id_type=MESH,
        )

    def seat(source, target):
        other = (source % lanes + lanes - target % lanes) % lanes
        return other * experts + source // lanes

    def dispatch(target, place, m, q, peer):
        columns = pl.ds(q * part, part)
        return pltpu.make_async_remote_copy(
            send.at[place, m, peer // lanes, :, columns], recv.at[m, seat(me, peer), :, columns],
            disp_send.at[place, m, q], disp_recv.at[m, q, seat(me, peer)],
            device_id=(target, peer), device_id_type=MESH,
        )

    def arrived(m, q, place):
        block = recv.at[m, place, :, pl.ds(q * part, part)]
        return pltpu.make_async_copy(block, block, disp_recv.at[m, q, place])

    def keep(m, q):
        columns = pl.ds(q * part, part)
        return pltpu.make_async_copy(
            send.at[FIRST, m, own_expert, :, columns], recv.at[m, own_expert, :, columns], disp_recv.at[m, q, own_expert]
        )

    def exchange(m, q):
        return pltpu.make_async_remote_copy(
            cross_out.at[m, q], cross_in.at[m, q], cross_send.at[m], cross_recv.at[m, q],
            device_id=(section, mate), device_id_type=MESH,
        )

    meet, meet_place = meeting(section)

    def give_back(m, q, plane):
        aside = one(section == 1) * (m % 2)
        return pltpu.make_async_remote_copy(
            back.at[m, q, plane], ret.at[meet_place, m, q, own_expert], ret_send.at[m],
            ret_recv.at[meet_place, m, q, own_expert],
            device_id=(meet + aside * (last - meet), plane * lanes + lane), device_id_type=MESH,
        )

    def stay(m, q):
        return pltpu.make_async_copy(
            back.at[m, q, own_expert], ret.at[1, m, q, own_expert], ret_recv.at[1, m, q, own_expert]
        )

    def returned(place, m, q, e):
        block = ret.at[place, m, q, e]
        return pltpu.make_async_copy(block, block, ret_recv.at[place, m, q, e])

    def result(m, target, i, source=SUM):
        return pltpu.make_async_remote_copy(
            rows.at[source, m], rows.at[START, m], out_send.at[i, m], out_recv.at[m], device_id=(target, me), device_id_type=MESH,
        )

    def landed(m):
        return pltpu.make_async_copy(rows.at[START, m], rows.at[START, m], out_recv.at[m])

    def gone(place, m, q, count=n):
        block = recv.at[m, pl.ds(0, count), :, pl.ds(q * part, part)]
        pltpu.make_async_copy(block, block, disp_send.at[place, m, q]).wait()

    def send_rows(target, place, m, source, square, gain, selector, own=False):
        scale = lax.rsqrt(square / width + 1e-06)
        for q in range(PARTS):
            if not place:
                @pl.when((m > 0) & (section > 0))
                def _():
                    for r in (range(PARTS) if q == 0 else ()):
                        gone(place, m - 1, r)

            columns = slice(q * part, (q + 1) * part)
            normed = (rows[source, m, :, columns].astype(F32) * scale * gain[:, columns]).astype(BF16)
            packed = jnp.dot(selector, normed, preferred_element_type=F32).astype(BF16)
            for e in range(experts):
                send[place, m, e, :, columns] = packed[e * cap:(e + 1) * cap]
            for peer in peers:
                dispatch(target, place, m, q, peer).start()
            if own:
                keep(m, q).start()
            else:
                dispatch(target, place, m, q, me).start()

    def first_rows(m, gain, selector, own):
        entry(m).wait()
        x = rows[ENTRY, m].astype(F32)
        send_rows(0, FIRST, m, ENTRY, jnp.sum(x * x, axis=-1, keepdims=True), gain, selector, own)

    def gate_up(m):
        g = jnp.zeros((n * cap, hidden), F32)
        u = jnp.zeros((n * cap, hidden), F32)
        for q in range(PARTS):
            for place in range(n):
                arrived(m, q, place).wait()
            if q == 1:
                @pl.when((section == 0) & (m < HERE - 1))
                def _():
                    first_rows(m + 1, gains_ref, pack_all[0, m + 1], True)
            columns = slice(q * part, (q + 1) * part)
            lhs = recv[m, :, :, columns].reshape(n * cap, part)
            g = g + jnp.dot(lhs, gate_w[columns, :], preferred_element_type=F32)
            u = u + jnp.dot(lhs, up_w[columns, :], preferred_element_type=F32)
        act[...] = (g / (1.0 + jnp.exp(-g)) * u).astype(BF16)

    def down(m):
        for q in range(PARTS):
            columns = slice(q * part, (q + 1) * part)
            y = jnp.dot(act[...], down_w[:, columns], preferred_element_type=F32)
            mine[q] = y[: experts * cap]
            for p in range(experts):
                cross_out[m, q, p] = y[(experts + p) * cap:(experts + p + 1) * cap].astype(BF16)
            exchange(m, q).start()

    def pair(m):
        for q in range(PARTS):
            exchange(m, q).wait_recv()
            both = (mine[q] + cross_in[m, q].reshape(experts * cap, part).astype(F32)).astype(BF16)
            for p in range(experts):
                back[m, q, p] = both[p * cap:(p + 1) * cap]
            for plane in planes[:-1]:
                give_back(m, q, plane).start()

            @pl.when(section == last)
            def _():
                stay(m, q).start()

            @pl.when(section < last)
            def _():
                give_back(m, q, own_expert).start()

    def gates(layer, source, m):
        x = rows[source, m].astype(F32)
        scale = lax.rsqrt(jnp.mean(x * x, axis=-1, keepdims=True) + 1e-06)
        normed = (x * scale * gains_all[layer]).astype(BF16)
        logits = lax.dot_general(normed, router_all[layer], (((1,), (1,)), ((), ())), preferred_element_type=F32)
        scores = jax.nn.sigmoid(logits)
        col = lax.broadcasted_iota(jnp.int32, (tok, 128), 1)
        spread = jnp.zeros((tok, 128), F32)
        for e in range(experts):
            spread = jnp.where(col // cap == e, scores[:, e:e + 1], spread)
        chosen = spread * place_all[layer, m]
        weight = 2.5 * chosen / jnp.sum(chosen, axis=1, keepdims=True)
        high = weight.astype(BF16).astype(F32)
        return jnp.concatenate([high, weight - high], axis=0)[:, : experts * cap].astype(BF16)

    def combine(place, source, m, weight, final, into=SUM):
        square = jnp.zeros((tok, 1), F32)
        for q in range(PARTS):
            for e in range(experts):
                returned(place, m, q, e).wait()
            columns = slice(q * part, (q + 1) * part)
            y = jnp.dot(weight, ret[place, m, q].reshape(experts * cap, part), preferred_element_type=F32)
            x = rows[source, m, :, columns].astype(F32)
            z = (x + (y[:tok] + y[tok:])).astype(BF16)
            if final:
                rows[ENTRY, m, :, columns] = z
            else:
                rows[into, m, :, columns] = z
                z = z.astype(F32)
                square = square + jnp.sum(z * z, axis=-1, keepdims=True)
        return square

    def finish_aside(m):
        square = combine(0, SUM, m, gates(1, SUM, m), False, EXTRA)
        send_rows(2, ASIDE, m, EXTRA, square, gains_all[2], pack_all[2, m])
        result(m, 1, 1, EXTRA).start()

    def finish(layer, source, m):
        weight = gates(layer, source, m)
        square = combine(0, source, m, weight, False)
        send_rows(layer + 1, 0, m, SUM, square, gains_all[layer + 1], pack_all[layer + 1, m])
        result(m, layer, 0).start()

        @pl.when(layer == last - 1)
        def _():
            result(m, last, 1).start()

    def leave(place, m):
        return pltpu.make_async_copy(rows.at[place, m], out_ref.at[m], entry_sem.at[m])

    def final(m):
        landed(m).wait()
        combine(1, START, m, gates(last, START, m), True)
        leave(ENTRY, m).start()

    def left(ref, semaphore):
        pltpu.make_async_copy(ref, ref, semaphore).wait()

    def sent(m):
        left(cross_out.at[m], cross_send.at[m])

        @pl.when(section < last)
        def _():
            left(back.at[m], ret_send.at[m])

        @pl.when(section == last)
        def _():
            left(recv.at[m, pl.ds(0, experts - 1)], ret_send.at[m])

    def load():
        for peer in peers:
            count_copy(me, peer, 0).wait_recv()
        hot = hot_ref[...]
        slot_expert = lax.broadcasted_iota(jnp.int32, (1, 128), 1) // cap
        total = jnp.sum(counts_in[:, 0, :], axis=0, keepdims=True)
        home = jnp.sum(jnp.where(slot_expert == own_expert, total, 0.0), axis=1, keepdims=True)
        extra = jnp.sum(jnp.where(slot_expert == hot // BLOCKS_PER_EXPERT, counts[0:1, :], 0.0), axis=1, keepdims=True)
        share = jnp.where(hot // (BLOCKS_PER_EXPERT // lanes) == me, 1.0, 2.0)
        load_ref[...] = (home * share + extra) / float(micro * tok * top * BLOCKS_PER_EXPERT)
        for order, peer in enumerate(peers):
            count_copy(peer, me, order).wait_send()

    @pl.when(section == 0)
    def _():
        first_rows(0, gains_ref, pack_all[0, 0], True)

    held = jnp.zeros((1, 128), F32)
    for m in range(micro):
        place = placement(m, 128).T
        place_all[section, m] = place
        held = held + jnp.sum(place, axis=0, keepdims=True)
    counts[...] = jnp.broadcast_to(held, counts.shape)
    gains_all[section] = gains_ref[...]
    router_all[section] = router_ref[...]

    def params(act_on):
        @pl.when(section < 2)
        def _():
            for i in range(4):
                act_on(param(i, last, section, 0))

        @pl.when(section >= 2)
        def _():
            for i in range(4):
                act_on(param(i, section - 2, section, 0))

        @pl.when((section >= 1) & (section < last))
        def _():
            for i in range(4):
                act_on(param(i, section - 1, section, 1))

        @pl.when(section == 2)
        def _():
            for i in range(4):
                act_on(param(i, last, section, 2))

    params(lambda copy: copy.start())

    for order, peer in enumerate(peers):
        count_copy(peer, me, order).start()
    counts_in[me] = counts[...]

    @pl.when(section == last)
    def _():
        for layer in range(3):
            for i in range(4):
                param(i, 0, layer, 0).wait_recv()

        def begin(m, carry):
            first_rows(m, gains_all[0], pack_all[0, m], False)
            return carry

        lax.fori_loop(HERE, micro, begin, 0)
        for m in range(HERE):
            entry(m).wait()

        def turn(m, carry):
            finish(0, ENTRY, m)
            return carry

        lax.fori_loop(0, micro, turn, 0)

        def turn_aside(i, carry):
            finish_aside(2 * i + 1)
            return carry

        lax.fori_loop(0, micro // 2, turn_aside, 0)

    weights[0].wait()
    weights[1].wait()

    gate_up(0)
    eager = section >= 0

    def step(m, carry):
        @pl.when(m == 0)
        def _():
            weights[2].wait()

        down(m)

        @pl.when(m == 0)
        def _():
            load()

        @pl.when((m < micro - 1) & eager)
        def _():
            gate_up(m + 1)

        pair(m)

        @pl.when((m < micro - 1) & jnp.logical_not(eager))
        def _():
            gate_up(m + 1)

        @pl.when(m > 0)
        def _():
            sent(m - 1)

            @pl.when(section == last)
            def _():
                final(m - 1)

        return carry

    lax.fori_loop(0, micro, step, 0)

    def settle():
        params(lambda copy: copy.wait_send())

        @pl.when((section != last - 1) & (section > 0))
        def _():
            for q in range(PARTS):
                gone(0, micro - 1, q)

        def drain(m, carry):
            @pl.when((section != last - 1) & ((section > 0) | (m % 2 == 0)))
            def _():
                result(m, section, 0).wait_send()

            @pl.when((section == 0) & (m % 2 == 0))
            def _():
                for q in range(PARTS):
                    gone(0, m, q)

            @pl.when((section == last) & (m % 2 == 1))
            def _():
                result(m, 1, 1, EXTRA).wait_send()
                for q in range(PARTS):
                    gone(ASIDE, m, q)

            @pl.when(section == last - 2)
            def _():
                result(m, section, 1).wait_send()

            @pl.when((section == 0) & (m < HERE))
            def _():
                for q in range(PARTS):
                    gone(FIRST, m, q, n - 1)

            @pl.when((section == last) & (m >= HERE))
            def _():
                for q in range(PARTS):
                    gone(FIRST, m, q)

            return carry

        lax.fori_loop(0, micro, drain, 0)

    @pl.when(section == last)
    def _():
        settle()
        final(micro - 1)

    @pl.when(section < last - 1)
    def _():
        for i in range(4):
            param(i, 0, section + 1, 0).wait_recv()
            param(i, 0, section + 2, 0).wait_recv()

        def turn(m, carry):
            landed(m).wait()
            leave(START, m).start()

            @pl.when((section > 0) | (m % 2 == 0))
            def _():
                finish(section + 1, START, m)

            return carry

        lax.fori_loop(0, micro, turn, 0)

    @pl.when(section == last - 1)
    def _():
        def take(m, carry):
            landed(m).wait()
            leave(START, m).start()
            return carry

        lax.fori_loop(0, micro, take, 0)

    @pl.when(section < last)
    def _():
        sent(micro - 1)
        settle()

    @pl.when(section == last)
    def _():
        sent(micro - 1)

    for m in range(micro):
        leave(START, m).wait()


def local(sections, n, rows_in, routes, hot_blocks, gains, router, w_gate, w_up, w_down):
    micro, tok, width = rows_in.shape
    experts, hidden, top = router.shape[2], w_gate.shape[2], routes.shape[3]
    cap, part = tok // 2, width // PARTS
    vmem = pl.BlockSpec(memory_space=pltpu.VMEM)
    hbm = pl.BlockSpec(memory_space=pl.ANY)
    dma = pltpu.SemaphoreType.DMA
    out, load = pl.pallas_call(
        functools.partial(kernel, sections, n, experts, top),
        out_shape=(jax.ShapeDtypeStruct((micro, tok, width), BF16), jax.ShapeDtypeStruct((1, 1), F32)),
        in_specs=[hbm, vmem, vmem, vmem, vmem, hbm, hbm, hbm],
        out_specs=(hbm, vmem),
        scratch_shapes=[
            pltpu.VMEM((width, hidden), BF16),
            pltpu.VMEM((width, hidden), BF16),
            pltpu.VMEM((hidden, width), BF16),
            pltpu.VMEM((4, micro, tok, width), BF16),
            pltpu.VMEM((3, micro, experts, cap, width), BF16),
            pltpu.VMEM((micro, n, cap, width), BF16),
            pltpu.VMEM((PARTS, experts * cap, part), F32),
            pltpu.VMEM((micro, PARTS, experts, cap, part), BF16),
            pltpu.VMEM((micro, PARTS, experts, cap, part), BF16),
            pltpu.VMEM((micro, PARTS, experts, cap, part), BF16),
            pltpu.VMEM((2, micro, PARTS, experts, cap, part), BF16),
            pltpu.VMEM((sections, 1, width), F32),
            pltpu.VMEM((sections, experts, width), BF16),
            pltpu.VMEM((sections, micro, tok, 128), F32),
            pltpu.VMEM((sections, micro, experts * cap, tok), BF16),
            pltpu.VMEM((n * cap, hidden), BF16),
            pltpu.VMEM((8, 128), F32),
            pltpu.VMEM((n, 8, 128), F32),
            dma((3,)), dma((micro,)), dma((2, micro)), dma((micro,)),
            dma((3, micro, PARTS)), dma((micro, PARTS, n)), dma((micro,)), dma((micro, PARTS)),
            dma((micro,)), dma((2, micro, PARTS, experts)), dma((n,)), dma((n,)),
            dma((3, 4)), dma((sections, 4)),
        ],
        compiler_params=pltpu.CompilerParams(collective_id=0, has_side_effects=True, vmem_limit_bytes=60 * 1024 * 1024),
    )(
        rows_in, jnp.swapaxes(routes[0], 1, 2), hot_blocks.reshape(1, 1), gains, router[0].T, w_gate[0], w_up[0], w_down[0],
    )
    return out[None], load


def solution(mesh):
    body = functools.partial(local, mesh.shape["section"], mesh.shape["ep"])
    return jax.shard_map(
        body,
        mesh=mesh,
        in_specs=(
            P(None, "ep", None),
            P("section", None, "ep", None),
            P("section"),
            P("section", None),
            P("section", None, None),
            P("section", None, "ep"),
            P("section", None, "ep"),
            P("section", "ep", None),
        ),
        out_specs=(P("section", None, "ep", None), P("section", "ep")),
        check_vma=False,
    )
```

```python
import functools

import jax
import jax.numpy as jnp
from jax import lax
from jax.experimental import pallas as pl
from jax.experimental.pallas import tpu as pltpu
from jax.sharding import PartitionSpec as P

BLOCKS_PER_EXPERT = 4
PARTS = 4
START, ENTRY, SUM, EXTRA = range(4)
FIRST, ASIDE = 1, 2
HERE = 2
MESH = pl.DeviceIdType.MESH
F32 = jnp.float32
BF16 = jnp.bfloat16


def flip(index, mask, count):
    result, bit = 0, 1
    while bit < count:
        digit = (index // bit) % 2
        result = result + bit * ((1 - digit) if mask & bit else digit)
        bit *= 2
    return result


def kernel(
    sections, n, experts, top,
    rows_hbm, routes_ref, hot_ref, gains_ref, router_ref, gate_hbm, up_hbm, down_hbm,
    out_ref, load_ref,
    gate_w, up_w, down_w, rows, send, recv, mine, cross_out, cross_in, back, ret,
    gains_all, router_all, place_all, pack_all, act, counts, counts_in,
    weight_sem, entry_sem, out_send, out_recv, disp_send, disp_recv, cross_send, cross_recv,
    ret_send, ret_recv, count_send, count_recv, param_send, param_recv,
):
    _, micro, tok, width = rows.shape
    cap = tok // 2
    lanes = n // experts
    hidden = gate_w.shape[1]
    part = width // PARTS
    last = sections - 1
    section = lax.axis_index("section")
    me = lax.axis_index("ep")
    own_expert, lane = me // lanes, me % lanes
    mate = own_expert * lanes + (1 - lane)
    everyone = [flip(me, mask, n) for mask in range(n - 1, -1, -1)]
    peers = everyone[:-1]
    planes = [flip(own_expert, mask, experts) for mask in range(experts - 1, -1, -1)]

    def one(condition):
        return condition.astype(jnp.int32)

    def meeting(layer):
        edge = one(layer == 0) + one(layer == last)
        return edge * last + (1 - edge) * (layer - 1), one(layer == last)

    weights = [
        pltpu.make_async_copy(source, target, weight_sem.at[i])
        for i, (source, target) in enumerate(((gate_hbm, gate_w), (up_hbm, up_w), (down_hbm, down_w)))
    ]

    def entry(m):
        return pltpu.make_async_copy(rows_hbm.at[m], rows.at[ENTRY, m], entry_sem.at[m])

    @pl.when(section == 0)
    def _():
        for m in range(HERE):
            entry(m).start()

    @pl.when(section == last)
    def _():
        for m in range(micro):
            entry(m).start()

    for copy in weights:
        copy.start()

    barrier = pltpu.get_barrier_semaphore()
    for peer in peers:
        pl.semaphore_signal(barrier, inc=1, device_id=(section, peer), device_id_type=MESH)
    partners = 0
    for other in range(sections):
        linked = (section == other - 2) | (section == other + 2)
        if other < last:
            linked = linked | (section == other - 1)
        if other < last - 1:
            linked = linked | (section == other + 1)
        if other < 3:
            linked = linked | (section == last)
        if other == last:
            linked = linked | (section < 3)
        linked = linked & (section != other)
        partners = partners + one(linked)

        @pl.when(linked)
        def _():
            for peer in everyone:
                pl.semaphore_signal(barrier, inc=1, device_id=(other, peer), device_id_type=MESH)

    def placement(m, count):
        slot = lax.broadcasted_iota(jnp.int32, (count, tok), 0)
        expert, rank = slot // cap, slot % cap
        routed = (routes_ref[m, 0:1, :] == expert) | (routes_ref[m, 1:2, :] == expert)
        earlier = (
            lax.broadcasted_iota(jnp.int32, (tok, tok), 0) < lax.broadcasted_iota(jnp.int32, (tok, tok), 1)
        ).astype(BF16)
        taken = jnp.dot(routed.astype(BF16), earlier, preferred_element_type=F32)
        return jnp.where(routed & (taken == rank.astype(F32)), 1.0, 0.0)

    for m in range(micro):
        pack_all[section, m] = placement(m, experts * cap).astype(BF16)

    pl.semaphore_wait(barrier, n - 1 + n * partners)

    def param(i, target, layer, way):
        ref = (gains_all, router_all, place_all, pack_all)[i]
        return pltpu.make_async_remote_copy(
            ref.at[layer], ref.at[layer], param_send.at[way, i], param_recv.at[layer, i],
            device_id=(target, me), device_id_type=MESH,
        )

    def count_copy(peer, source, order):
        return pltpu.make_async_remote_copy(
            counts, counts_in.at[source], count_send.at[order], count_recv.at[source],
            device_id=(section, peer), device_id_type=MESH,
        )

    def seat(source, target):
        other = (source % lanes + lanes - target % lanes) % lanes
        return other * experts + source // lanes

    def dispatch(target, place, m, q, peer):
        columns = pl.ds(q * part, part)
        return pltpu.make_async_remote_copy(
            send.at[place, m, peer // lanes, :, columns], recv.at[m, seat(me, peer), :, columns],
            disp_send.at[place, m, q], disp_recv.at[m, q, seat(me, peer)],
            device_id=(target, peer), device_id_type=MESH,
        )

    def arrived(m, q, place):
        block = recv.at[m, place, :, pl.ds(q * part, part)]
        return pltpu.make_async_copy(block, block, disp_recv.at[m, q, place])

    def keep(m, q):
        columns = pl.ds(q * part, part)
        return pltpu.make_async_copy(
            send.at[FIRST, m, own_expert, :, columns], recv.at[m, own_expert, :, columns], disp_recv.at[m, q, own_expert]
        )

    def exchange(m, q):
        return pltpu.make_async_remote_copy(
            cross_out.at[m, q], cross_in.at[m, q], cross_send.at[m], cross_recv.at[m, q],
            device_id=(section, mate), device_id_type=MESH,
        )

    meet, meet_place = meeting(section)

    def give_back(m, q, plane):
        aside = one(section == 1) * (m % 2)
        return pltpu.make_async_remote_copy(
            back.at[m, q, plane], ret.at[meet_place, m, q, own_expert], ret_send.at[m],
            ret_recv.at[meet_place, m, q, own_expert],
            device_id=(meet + aside * (last - meet), plane * lanes + lane), device_id_type=MESH,
        )

    def stay(m, q):
        return pltpu.make_async_copy(
            back.at[m, q, own_expert], ret.at[1, m, q, own_expert], ret_recv.at[1, m, q, own_expert]
        )

    def returned(place, m, q, e):
        block = ret.at[place, m, q, e]
        return pltpu.make_async_copy(block, block, ret_recv.at[place, m, q, e])

    def result(m, target, i, source=SUM):
        return pltpu.make_async_remote_copy(
            rows.at[source, m], rows.at[START, m], out_send.at[i, m], out_recv.at[m], device_id=(target, me), device_id_type=MESH,
        )

    def landed(m):
        return pltpu.make_async_copy(rows.at[START, m], rows.at[START, m], out_recv.at[m])

    def gone(place, m, q, count=n):
        block = recv.at[m, pl.ds(0, count), :, pl.ds(q * part, part)]
        pltpu.make_async_copy(block, block, disp_send.at[place, m, q]).wait()

    def send_rows(target, place, m, source, square, gain, selector, own=False):
        scale = lax.rsqrt(square / width + 1e-06)
        for q in range(PARTS):
            if not place:
                @pl.when((m > 0) & (section > 0))
                def _():
                    for r in (range(PARTS) if q == 0 else ()):
                        gone(place, m - 1, r)

            columns = slice(q * part, (q + 1) * part)
            normed = (rows[source, m, :, columns].astype(F32) * scale * gain[:, columns]).astype(BF16)
            packed = jnp.dot(selector, normed, preferred_element_type=F32).astype(BF16)
            for e in range(experts):
                send[place, m, e, :, columns] = packed[e * cap:(e + 1) * cap]
            for peer in peers:
                dispatch(target, place, m, q, peer).start()
            if own:
                keep(m, q).start()
            else:
                dispatch(target, place, m, q, me).start()

    def first_rows(m, gain, selector, own):
        entry(m).wait()
        x = rows[ENTRY, m].astype(F32)
        send_rows(0, FIRST, m, ENTRY, jnp.sum(x * x, axis=-1, keepdims=True), gain, selector, own)

    def gate_up(m):
        g = jnp.zeros((n * cap, hidden), F32)
        u = jnp.zeros((n * cap, hidden), F32)
        for q in range(PARTS):
            for place in range(n):
                arrived(m, q, place).wait()
            if q == 1:
                @pl.when((section == 0) & (m < HERE - 1))
                def _():
                    first_rows(m + 1, gains_ref, pack_all[0, m + 1], True)
            columns = slice(q * part, (q + 1) * part)
            lhs = recv[m, :, :, columns].reshape(n * cap, part)
            g = g + jnp.dot(lhs, gate_w[columns, :], preferred_element_type=F32)
            u = u + jnp.dot(lhs, up_w[columns, :], preferred_element_type=F32)
        act[...] = (g / (1.0 + jnp.exp(-g)) * u).astype(BF16)

    def down(m):
        for q in range(PARTS):
            columns = slice(q * part, (q + 1) * part)
            y = jnp.dot(act[...], down_w[:, columns], preferred_element_type=F32)
            mine[q] = y[: experts * cap]
            for p in range(experts):
                cross_out[m, q, p] = y[(experts + p) * cap:(experts + p + 1) * cap].astype(BF16)
            exchange(m, q).start()

    def pair(m):
        for q in range(PARTS):
            exchange(m, q).wait_recv()
            both = (mine[q] + cross_in[m, q].reshape(experts * cap, part).astype(F32)).astype(BF16)
            for p in range(experts):
                back[m, q, p] = both[p * cap:(p + 1) * cap]
            for plane in planes[:-1]:
                give_back(m, q, plane).start()

            @pl.when(section == last)
            def _():
                stay(m, q).start()

            @pl.when(section < last)
            def _():
                give_back(m, q, own_expert).start()

    def gates(layer, source, m):
        x = rows[source, m].astype(F32)
        scale = lax.rsqrt(jnp.mean(x * x, axis=-1, keepdims=True) + 1e-06)
        normed = (x * scale * gains_all[layer]).astype(BF16)
        logits = lax.dot_general(normed, router_all[layer], (((1,), (1,)), ((), ())), preferred_element_type=F32)
        scores = jax.nn.sigmoid(logits)
        col = lax.broadcasted_iota(jnp.int32, (tok, 128), 1)
        spread = jnp.zeros((tok, 128), F32)
        for e in range(experts):
            spread = jnp.where(col // cap == e, scores[:, e:e + 1], spread)
        chosen = spread * place_all[layer, m]
        weight = 2.5 * chosen / jnp.sum(chosen, axis=1, keepdims=True)
        high = weight.astype(BF16).astype(F32)
        return jnp.concatenate([high, weight - high], axis=0)[:, : experts * cap].astype(BF16)

    def combine(place, source, m, weight, final, into=SUM):
        square = jnp.zeros((tok, 1), F32)
        for q in range(PARTS):
            for e in range(experts):
                returned(place, m, q, e).wait()
            columns = slice(q * part, (q + 1) * part)
            y = jnp.dot(weight, ret[place, m, q].reshape(experts * cap, part), preferred_element_type=F32)
            x = rows[source, m, :, columns].astype(F32)
            z = (x + (y[:tok] + y[tok:])).astype(BF16)
            if final:
                rows[ENTRY, m, :, columns] = z
            else:
                rows[into, m, :, columns] = z
                z = z.astype(F32)
                square = square + jnp.sum(z * z, axis=-1, keepdims=True)
        return square

    def finish_aside(m):
        square = combine(0, SUM, m, gates(1, SUM, m), False, EXTRA)
        send_rows(2, ASIDE, m, EXTRA, square, gains_all[2], pack_all[2, m])
        result(m, 1, 1, EXTRA).start()

    def finish(layer, source, m):
        weight = gates(layer, source, m)
        square = combine(0, source, m, weight, False)
        send_rows(layer + 1, 0, m, SUM, square, gains_all[layer + 1], pack_all[layer + 1, m])
        result(m, layer, 0).start()

        @pl.when(layer == last - 1)
        def _():
            result(m, last, 1).start()

    def leave(place, m):
        return pltpu.make_async_copy(rows.at[place, m], out_ref.at[m], entry_sem.at[m])

    def final(m):
        landed(m).wait()
        combine(1, START, m, gates(last, START, m), True)
        leave(ENTRY, m).start()

    def left(ref, semaphore):
        pltpu.make_async_copy(ref, ref, semaphore).wait()

    def sent(m):
        left(cross_out.at[m], cross_send.at[m])

        @pl.when(section < last)
        def _():
            left(back.at[m], ret_send.at[m])

        @pl.when(section == last)
        def _():
            left(recv.at[m, pl.ds(0, experts - 1)], ret_send.at[m])

    def load():
        for peer in peers:
            count_copy(me, peer, 0).wait_recv()
        hot = hot_ref[...]
        slot_expert = lax.broadcasted_iota(jnp.int32, (1, 128), 1) // cap
        total = jnp.sum(counts_in[:, 0, :], axis=0, keepdims=True)
        home = jnp.sum(jnp.where(slot_expert == own_expert, total, 0.0), axis=1, keepdims=True)
        extra = jnp.sum(jnp.where(slot_expert == hot // BLOCKS_PER_EXPERT, counts[0:1, :], 0.0), axis=1, keepdims=True)
        share = jnp.where(hot // (BLOCKS_PER_EXPERT // lanes) == me, 1.0, 2.0)
        load_ref[...] = (home * share + extra) / float(micro * tok * top * BLOCKS_PER_EXPERT)
        for order, peer in enumerate(peers):
            count_copy(peer, me, order).wait_send()

    @pl.when(section == 0)
    def _():
        first_rows(0, gains_ref, pack_all[0, 0], True)

    held = jnp.zeros((1, 128), F32)
    for m in range(micro):
        place = placement(m, 128).T
        place_all[section, m] = place
        held = held + jnp.sum(place, axis=0, keepdims=True)
    counts[...] = jnp.broadcast_to(held, counts.shape)
    gains_all[section] = gains_ref[...]
    router_all[section] = router_ref[...]

    def params(act_on):
        @pl.when(section < 2)
        def _():
            for i in range(4):
                act_on(param(i, last, section, 0))

        @pl.when(section >= 2)
        def _():
            for i in range(4):
                act_on(param(i, section - 2, section, 0))

        @pl.when((section >= 1) & (section < last))
        def _():
            for i in range(4):
                act_on(param(i, section - 1, section, 1))

        @pl.when(section == 2)
        def _():
            for i in range(4):
                act_on(param(i, last, section, 2))

    params(lambda copy: copy.start())

    for order, peer in enumerate(peers):
        count_copy(peer, me, order).start()
    counts_in[me] = counts[...]

    @pl.when(section == last)
    def _():
        for layer in range(3):
            for i in range(4):
                param(i, 0, layer, 0).wait_recv()

        def begin(m, carry):
            first_rows(m, gains_all[0], pack_all[0, m], False)
            return carry

        lax.fori_loop(HERE, micro, begin, 0)
        for m in range(HERE):
            entry(m).wait()

        def turn(m, carry):
            finish(0, ENTRY, m)
            return carry

        lax.fori_loop(0, micro, turn, 0)

        def turn_aside(i, carry):
            finish_aside(2 * i + 1)
            return carry

        lax.fori_loop(0, micro // 2, turn_aside, 0)

    weights[0].wait()
    weights[1].wait()

    gate_up(0)

    def step(m, carry):
        @pl.when(m == 0)
        def _():
            weights[2].wait()

        down(m)

        @pl.when(m == 0)
        def _():
            load()

        @pl.when((m < micro - 1) & ((section == 0) | (m > 0)))
        def _():
            gate_up(m + 1)

        pair(m)

        @pl.when((m < micro - 1) & jnp.logical_not((section == 0) | (m > 0)))
        def _():
            gate_up(m + 1)

        @pl.when(m > 0)
        def _():
            sent(m - 1)

            @pl.when(section == last)
            def _():
                final(m - 1)

        return carry

    lax.fori_loop(0, micro, step, 0)

    def settle():
        params(lambda copy: copy.wait_send())

        @pl.when((section != last - 1) & (section > 0))
        def _():
            for q in range(PARTS):
                gone(0, micro - 1, q)

        def drain(m, carry):
            @pl.when((section != last - 1) & ((section > 0) | (m % 2 == 0)))
            def _():
                result(m, section, 0).wait_send()

            @pl.when((section == 0) & (m % 2 == 0))
            def _():
                for q in range(PARTS):
                    gone(0, m, q)

            @pl.when((section == last) & (m % 2 == 1))
            def _():
                result(m, 1, 1, EXTRA).wait_send()
                for q in range(PARTS):
                    gone(ASIDE, m, q)

            @pl.when(section == last - 2)
            def _():
                result(m, section, 1).wait_send()

            @pl.when((section == 0) & (m < HERE))
            def _():
                for q in range(PARTS):
                    gone(FIRST, m, q, n - 1)

            @pl.when((section == last) & (m >= HERE))
            def _():
                for q in range(PARTS):
                    gone(FIRST, m, q)

            return carry

        lax.fori_loop(0, micro, drain, 0)

    @pl.when(section == last)
    def _():
        settle()
        final(micro - 1)

    @pl.when(section < last - 1)
    def _():
        for i in range(4):
            param(i, 0, section + 1, 0).wait_recv()
            param(i, 0, section + 2, 0).wait_recv()

        def turn(m, carry):
            landed(m).wait()
            leave(START, m).start()

            @pl.when((section > 0) | (m % 2 == 0))
            def _():
                finish(section + 1, START, m)

            return carry

        lax.fori_loop(0, micro, turn, 0)

    @pl.when(section == last - 1)
    def _():
        def take(m, carry):
            landed(m).wait()
            leave(START, m).start()
            return carry

        lax.fori_loop(0, micro, take, 0)

    @pl.when(section < last)
    def _():
        sent(micro - 1)
        settle()

    @pl.when(section == last)
    def _():
        sent(micro - 1)

    for m in range(micro):
        leave(START, m).wait()


def local(sections, n, rows_in, routes, hot_blocks, gains, router, w_gate, w_up, w_down):
    micro, tok, width = rows_in.shape
    experts, hidden, top = router.shape[2], w_gate.shape[2], routes.shape[3]
    cap, part = tok // 2, width // PARTS
    vmem = pl.BlockSpec(memory_space=pltpu.VMEM)
    hbm = pl.BlockSpec(memory_space=pl.ANY)
    dma = pltpu.SemaphoreType.DMA
    out, load = pl.pallas_call(
        functools.partial(kernel, sections, n, experts, top),
        out_shape=(jax.ShapeDtypeStruct((micro, tok, width), BF16), jax.ShapeDtypeStruct((1, 1), F32)),
        in_specs=[hbm, vmem, vmem, vmem, vmem, hbm, hbm, hbm],
        out_specs=(hbm, vmem),
        scratch_shapes=[
            pltpu.VMEM((width, hidden), BF16),
            pltpu.VMEM((width, hidden), BF16),
            pltpu.VMEM((hidden, width), BF16),
            pltpu.VMEM((4, micro, tok, width), BF16),
            pltpu.VMEM((3, micro, experts, cap, width), BF16),
            pltpu.VMEM((micro, n, cap, width), BF16),
            pltpu.VMEM((PARTS, experts * cap, part), F32),
            pltpu.VMEM((micro, PARTS, experts, cap, part), BF16),
            pltpu.VMEM((micro, PARTS, experts, cap, part), BF16),
            pltpu.VMEM((micro, PARTS, experts, cap, part), BF16),
            pltpu.VMEM((2, micro, PARTS, experts, cap, part), BF16),
            pltpu.VMEM((sections, 1, width), F32),
            pltpu.VMEM((sections, experts, width), BF16),
            pltpu.VMEM((sections, micro, tok, 128), F32),
            pltpu.VMEM((sections, micro, experts * cap, tok), BF16),
            pltpu.VMEM((n * cap, hidden), BF16),
            pltpu.VMEM((8, 128), F32),
            pltpu.VMEM((n, 8, 128), F32),
            dma((3,)), dma((micro,)), dma((2, micro)), dma((micro,)),
            dma((3, micro, PARTS)), dma((micro, PARTS, n)), dma((micro,)), dma((micro, PARTS)),
            dma((micro,)), dma((2, micro, PARTS, experts)), dma((n,)), dma((n,)),
            dma((3, 4)), dma((sections, 4)),
        ],
        compiler_params=pltpu.CompilerParams(collective_id=0, has_side_effects=True, vmem_limit_bytes=60 * 1024 * 1024),
    )(
        rows_in, jnp.swapaxes(routes[0], 1, 2), hot_blocks.reshape(1, 1), gains, router[0].T, w_gate[0], w_up[0], w_down[0],
    )
    return out[None], load


def solution(mesh):
    body = functools.partial(local, mesh.shape["section"], mesh.shape["ep"])
    return jax.shard_map(
        body,
        mesh=mesh,
        in_specs=(
            P(None, "ep", None),
            P("section", None, "ep", None),
            P("section"),
            P("section", None),
            P("section", None, None),
            P("section", None, "ep"),
            P("section", None, "ep"),
            P("section", "ep", None),
        ),
        out_specs=(P("section", None, "ep", None), P("section", "ep")),
        check_vma=False,
    )
```
